256 devices in a mesh: dp: 8 (over z), expert: 32 (over x, y, core).
Axes of the slice: x: 4, y: 4, z: 8, core: 2. Of those that a mesh axis runs over, the one named last changes fastest.
Arguments:
- tokens: bfloat16 [4096, 3584], P('expert', 'dp'), may hold values from -6 to 6
- cotangent: bfloat16 [4096, 3584], P('expert', 'dp'), may hold values from -6 to 6
- slot_ids: int32 [4096, 8], P('expert'), may hold values from 0 to 63, all different within a row; in each aligned block of 128 rows (0 to 127, 128 to 255, ...) at most 20 rows name the same one
- gates: float32 [4096, 8], P('expert'), may hold values from 0.05 to 1
- plan: int32 [32], replicated, may hold values from 0 to 31
- w_gate: bfloat16 [32, 3584, 1024], P('expert', 'dp'), may hold values from -0.09375 to 0.09375
- w_up: bfloat16 [32, 3584, 1024], P('expert', 'dp'), may hold values from -0.09375 to 0.09375
- w_down: bfloat16 [32, 1024, 3584], P('expert', None, 'dp'), may hold values from -0.1875 to 0.1875
Outputs:
- output: bfloat16 [4096, 3584], P('expert', 'dp')
- token_grad: bfloat16 [4096, 3584], P('expert', 'dp')
- grad_gate: float32 [32, 3584, 1024], P('expert', 'dp')
- grad_up: float32 [32, 3584, 1024], P('expert', 'dp')
- grad_down: float32 [32, 1024, 3584], P('expert', None, 'dp')
The draws below stay inside these ranges and needn't reach their ends.
Inputs may be any that keep to these rules, and one draw needn't show every extreme that they name: `slot_ids`: each row names 8 different slots. Within the 128 rows of one device no slot is named more than 20 times, a bound that some block reaches.
All inputs are finite; a program needn't handle non-finite values.
Results may differ from the reference program's by a relative error of at most 0.029.
Values may be sent and summed in bfloat16 or wider, within the bound.
A program may use at most 128 MiB of HBM per device.

```python
import math
import jax
import jax.numpy as jnp
import numpy as np
from jax import lax

D = 3584
H = 1024
TOPK = 8
TOK_DEV = 128
EXPERTS = 32
SLOTS = 64
CAP = 20
TOKENS = 4096
N_DP = 8
N_EXPERT = 32


def place_ends(values, stream_key, low, largest):
    index_at = [jax.random.randint(jax.random.fold_in(stream_key, axis), (), 0, length) for axis, length in enumerate(values.shape)]
    longest = values.shape.index(max(values.shape))
    next_to = index_at[:longest] + [(index_at[longest] + 1) % values.shape[longest]] + index_at[longest + 1:]
    return values.at[tuple(index_at)].set(low).at[tuple(next_to)].set(largest)


def level_of(own_key, shape, cuts, smallest, largest):
    loudness, own = 1.0, jax.random.fold_in(own_key, 6)
    for axis_at, shards_of in cuts:
        heights = jnp.exp(jax.random.uniform(jax.random.fold_in(own, axis_at), (shards_of,), jnp.float32, smallest / len(cuts), largest / len(cuts)))
        loudness = loudness * jnp.repeat(heights, shape[axis_at] // shards_of).reshape([-1 if axis == axis_at else 1 for axis in range(len(shape))])
    return loudness


def shared_out(stream_key, own, number, rows, amount, top, reach, slope):
    order = jax.random.permutation(stream_key, amount)
    packed, usual = load_shares(amount, rows * top, reach, slope, True), load_shares(amount, rows * top, reach, slope, False)
    places = jnp.arange(amount)

    def named(tallies, rotation):
        used = int((tallies > 0).sum())
        fixed = max(1, used // 4)
        passed = fixed + (places - fixed + rotation * (used - fixed)) % max(1, amount - fixed)
        return jnp.zeros((amount,), jnp.int32).at[order[jnp.where(places < fixed, places, passed)]].set(jnp.asarray(tallies, jnp.int32))

    tallies = jnp.where(number % 4 == 0, named(packed, number // 4), named(usual, number - number // 4 - 1))
    mixed = jax.random.permutation(jax.random.fold_in(own, 3), amount)
    giver, taker = mixed[0:amount // 2 * 2:2], mixed[1:amount // 2 * 2:2]
    room = jnp.minimum(tallies[giver] - 1, reach - tallies[taker]) // 2
    room = jnp.where((giver == order[0]) | (taker == order[0]) | (tallies[taker] == 0), 0, jnp.maximum(room, 0))
    passed = jax.random.randint(jax.random.fold_in(own, 4), (amount // 2,), 0, 1 << 20) % (room + 1)
    tallies = tallies.at[giver].add(-passed).at[taker].add(passed)
    members = jnp.searchsorted(jnp.cumsum(tallies), jnp.arange(rows * top), side="right").astype(jnp.int32)
    table = members.reshape(top, rows).T
    table = table[jax.random.permutation(jax.random.fold_in(own, 1), rows)]
    rotation = jax.random.randint(jax.random.fold_in(own, 2), (rows, 1), 0, top)
    return jnp.take_along_axis(table, (jnp.arange(top)[None, :] + rotation) % top, axis=1)


def load_shares(count, total, most, slope, full):
    loads = [(1 << 20) // math.isqrt(standing ** slope) + 1 for standing in range(1, count + 1)]
    largest = most if full else min(most, max(-(-total // count), total * loads[0] // sum(loads)))
    least = 1 if total - largest >= count - 1 else 0
    given, rest = [largest] + [least] * (count - 1), total - largest - least * (count - 1)
    while rest > 0:
        free = [i for i in range(1, count) if given[i] < largest] or [i for i in range(1, count) if given[i] < most]
        whole, budget = sum([loads[i] for i in free]), rest
        for i in free:
            addition = min(most - given[i], max(1, budget * loads[i] // whole), rest)
            given[i] = given[i] + addition
            rest = rest - addition
    return np.array(given)


def noise(rng, dims, deviation, limit, shards=(), held_as=jnp.bfloat16):
    array = deviation * jax.random.normal(rng, dims, jnp.float32)
    if shards:
        array = array * level_of(rng, dims, shards, -0.22, 0.18)
    return jnp.clip(array, -limit, limit).astype(held_as)


def setup_inputs(seed: int = 0) -> dict:
    key_list = jax.random.split(jax.random.key(seed), 9)
    tokens = noise(key_list[0], (TOKENS, D), 1.0, 6.0, ((0, 32), (1, 8)))
    cotangent = noise(key_list[1], (TOKENS, D), 1.0, 6.0, ((0, 32), (1, 8)))
    slot_ids_keys = jax.random.split(jax.random.fold_in(key_list[2], 1), TOKENS // TOK_DEV)
    slot_ids_turns = jax.random.permutation(jax.random.fold_in(key_list[2], 3), TOKENS // TOK_DEV)
    slot_ids = jax.vmap(lambda own, number: shared_out(jax.random.fold_in(key_list[2], 2), own, number, TOK_DEV, SLOTS, TOPK, CAP, 2))(slot_ids_keys, slot_ids_turns).reshape((TOKENS, TOPK))
    gates = jnp.clip(0.05 + 0.95 * jax.random.uniform(key_list[3], (TOKENS, TOPK), jnp.float32) ** level_of(key_list[3], (TOKENS, TOPK), ((0, 32),), -0.2, 0.2), 0.05, 1.0)
    plan = place_ends(jax.random.randint(key_list[4], (EXPERTS,), 0, EXPERTS), jax.random.fold_in(key_list[4], 1), 0, EXPERTS - 1).astype(jnp.int32)
    w_gate = noise(key_list[5], (EXPERTS, D, H), D ** -0.5, 0.09375, ((0, 32), (1, 8)))
    w_up = noise(key_list[6], (EXPERTS, D, H), D ** -0.5, 0.09375, ((0, 32), (1, 8)))
    w_down = noise(key_list[7], (EXPERTS, H, D), H ** -0.5, 0.1875, ((0, 32), (2, 8)))
    return dict(tokens=tokens, cotangent=cotangent, slot_ids=slot_ids, gates=gates, plan=plan, w_gate=w_gate, w_up=w_up, w_down=w_down)


def to_half(value):
    return lax.optimization_barrier(value.astype(jnp.bfloat16)).astype(jnp.float32)


def block_sum(left, right_blocks, form):
    row_total = left.shape[0]
    parts = jnp.einsum(form, left.reshape(row_total, N_DP, D // N_DP).astype(jnp.float32), right_blocks.astype(jnp.float32))
    return jnp.sum(to_half(parts), axis=1)


def slope_pair(grad, gate_sum, up_sum):
    sig = jax.nn.sigmoid(gate_sum)
    gate_slope = (grad * up_sum * sig * (1.0 + gate_sum * (1.0 - sig))).astype(jnp.bfloat16)
    up_slope = (grad * jax.nn.silu(gate_sum)).astype(jnp.bfloat16)
    return gate_slope, up_slope


def reference(tokens, cotangent, slot_ids, gates, plan, w_gate, w_up, w_down):
    per_device = TOK_DEV * TOPK
    row_total = N_EXPERT * CAP
    chosen = slot_ids.reshape(N_EXPERT, per_device).astype(jnp.int32)
    onehot = (chosen[:, :, None] == jnp.arange(SLOTS, dtype=jnp.int32)[None, None, :]).astype(jnp.int32)
    position = jnp.sum(jnp.cumsum(onehot, axis=1) * onehot, axis=2) - 1
    source = jnp.broadcast_to(jnp.arange(N_EXPERT, dtype=jnp.int32)[:, None], chosen.shape)
    choice_id = source * per_device + jnp.arange(per_device, dtype=jnp.int32)[None, :]
    flat_place = ((chosen * N_EXPERT + source) * CAP + position).reshape(-1).astype(jnp.int32)
    table = jnp.full((SLOTS * row_total,), TOKENS * TOPK, jnp.int32).at[flat_place].set(choice_id.reshape(-1)).reshape(SLOTS, row_total)
    tokens_pad = jnp.concatenate([tokens, jnp.zeros((1, D), tokens.dtype)])
    cot_pad = jnp.concatenate([cotangent, jnp.zeros((1, D), cotangent.dtype)])
    gate_pad = jnp.concatenate([gates.reshape(-1), jnp.zeros((1,), gates.dtype)])
    owner = jnp.concatenate([jnp.arange(EXPERTS, dtype=jnp.int32), plan.astype(jnp.int32)])

    def slot_work(slot):
        rows = table[slot]
        expert = owner[slot]
        token_rows = rows // TOPK
        x_rows = tokens_pad[token_rows]
        z_rows = (gate_pad[rows][:, None] * cot_pad[token_rows].astype(jnp.float32)).astype(jnp.bfloat16)
        gate_w = w_gate[expert]
        up_w = w_up[expert]
        down_w = w_down[expert]
        gate_sum = block_sum(x_rows, gate_w.reshape(N_DP, D // N_DP, H), "rak,akh->rah")
        up_sum = block_sum(x_rows, up_w.reshape(N_DP, D // N_DP, H), "rak,akh->rah")
        hidden = (jax.nn.silu(gate_sum) * up_sum).astype(jnp.bfloat16)
        expert_out = jnp.dot(hidden, down_w, preferred_element_type=jnp.float32).astype(jnp.bfloat16)
        hidden_grad = block_sum(z_rows, down_w.reshape(H, N_DP, D // N_DP), "rak,hak->rah")
        gate_slope, up_slope = slope_pair(hidden_grad, gate_sum, up_sum)
        back_out = (jnp.dot(gate_slope, gate_w.T, preferred_element_type=jnp.float32) + jnp.dot(up_slope, up_w.T, preferred_element_type=jnp.float32)).astype(jnp.bfloat16)
        grads = (jnp.dot(x_rows.T, gate_slope, preferred_element_type=jnp.float32), jnp.dot(x_rows.T, up_slope, preferred_element_type=jnp.float32), jnp.dot(hidden.T, z_rows, preferred_element_type=jnp.float32))
        return expert, expert_out, back_out, grads

    def replica_step(totals, slot):
        expert, expert_out, back_out, grads = slot_work(slot)
        totals = tuple(total.at[expert].add(to_half(grad)) for total, grad in zip(totals, grads))
        return totals, (expert_out, back_out)

    def home_step(totals, slot):
        expert, expert_out, back_out, grads = slot_work(slot)
        totals = tuple(total.at[expert].add(grad) for total, grad in zip(totals, grads))
        return totals, (expert_out, back_out)

    start = (jnp.zeros((EXPERTS, D, H), jnp.float32), jnp.zeros((EXPERTS, D, H), jnp.float32), jnp.zeros((EXPERTS, H, D), jnp.float32))
    totals, (rep_out, rep_back) = lax.scan(replica_step, start, jnp.arange(EXPERTS, SLOTS, dtype=jnp.int32))
    totals = tuple(to_half(total) for total in totals)
    totals, (home_out, home_back) = lax.scan(home_step, totals, jnp.arange(0, EXPERTS, dtype=jnp.int32))
    all_out = jnp.concatenate([home_out, rep_out]).reshape(SLOTS * row_total, D)
    all_back = jnp.concatenate([home_back, rep_back]).reshape(SLOTS * row_total, D)
    chosen_out = all_out[flat_place].astype(jnp.float32).reshape(TOKENS, TOPK, D)
    output = jnp.sum(gates[:, :, None] * chosen_out, axis=1).astype(jnp.bfloat16)
    chosen_back = all_back[flat_place].astype(jnp.float32).reshape(TOKENS, TOPK, D)
    token_grad = jnp.sum(chosen_back, axis=1).astype(jnp.bfloat16)
    return output, token_grad, totals[0], totals[1], totals[2]
```

```python
import functools

import jax
import jax.numpy as jnp
from jax import lax
from jax.experimental import pallas as pl
from jax.experimental.pallas import tpu as pltpu
from jax.sharding import PartitionSpec as P

MESH = pl.DeviceIdType.MESH
BF = jnp.bfloat16
F32 = jnp.float32
VMEM = pltpu.VMEM
DEPTH = 2
STRIDE = 11


def greet(axis, peers):
    barrier = pltpu.get_barrier_semaphore()
    for peer in peers:
        pl.semaphore_signal(barrier, inc=1, device_id={axis: peer}, device_id_type=MESH)


def greet_all(axis, count, me):
    barrier = pltpu.get_barrier_semaphore()

    def one(i, carry):
        pl.semaphore_signal(
            barrier, inc=1, device_id={axis: lax.rem(me + i, count)}, device_id_type=MESH
        )
        return carry

    lax.fori_loop(1, count, one, 0)


def each(count, first, function):
    def step(i, carry):
        function(i)
        return carry

    lax.fori_loop(first, count, step, 0)


def exchange_kernel(count, src, dst, send, recv, local):
    me = lax.axis_index("expert")
    greet_all("expert", count, me)
    pl.semaphore_wait(pltpu.get_barrier_semaphore(), count - 1)

    def copy(i):
        peer = lax.rem(me + STRIDE * i, count)
        return pltpu.make_async_remote_copy(
            src_ref=src.at[peer],
            dst_ref=dst.at[me],
            send_sem=send.at[i],
            recv_sem=recv.at[i],
            device_id={"expert": peer},
            device_id_type=MESH,
        )

    own = pltpu.make_async_copy(src.at[me], dst.at[me], local)
    own.start()
    each(count, 1, lambda i: copy(i).start())
    own.wait()
    each(count, 1, lambda i: copy(i).wait())


def exchange(blocks, collective_id):
    count = blocks.shape[0]
    return pl.pallas_call(
        functools.partial(exchange_kernel, count),
        out_shape=jax.ShapeDtypeStruct(blocks.shape, blocks.dtype),
        in_specs=[pl.BlockSpec(memory_space=VMEM)],
        out_specs=pl.BlockSpec(memory_space=VMEM),
        scratch_shapes=[
            pltpu.SemaphoreType.DMA((count,)),
            pltpu.SemaphoreType.DMA((count,)),
            pltpu.SemaphoreType.DMA,
        ],
        compiler_params=pltpu.CompilerParams(
            collective_id=collective_id, has_side_effects=True, vmem_limit_bytes=24 << 20
        ),
        name=f"exchange{collective_id}",
    )(blocks)


def stage_kernel(
    summing, count, ring, ints, flts, parts, source, acts, result,
    landed, held, staged, run, zs, zr, gs, gr, xs, xr, ys, yr, local,
):
    me = lax.axis_index("expert")
    z = lax.axis_index("dp")
    right, left = lax.rem(z + 1, ring), lax.rem(z + ring - 1, ring)
    chunk = parts.shape[1] // ring
    half = chunk // 2
    steps = ring // 2
    row_blocks = source.shape[0]
    lane_blocks = count // row_blocks
    piece = source.shape[2] // lane_blocks

    greet("dp", (right, left))
    greet_all("expert", count, me)
    pl.semaphore_wait(pltpu.get_barrier_semaphore(), count + 1)

    def rows_of(c, d=None):
        base = lax.rem(c + 2 * ring, ring) * chunk
        if d is None:
            return pl.ds(pl.multiple_of(base, chunk), chunk)
        return pl.ds(pl.multiple_of(base + d * half, half), half)

    def part_of(block):
        lane = pl.multiple_of(lax.rem(block, lane_blocks) * piece, piece)
        return (lax.div(block, lane_blocks), slice(None), pl.ds(lane, piece))

    def sum_copy(t, m, d):
        c = z + steps - t if d == 0 else z - steps + t
        if t == 0:
            src = parts.at[m, rows_of(c, d)]
            dst = landed.at[d, 0, m, pl.ds(d * half, half)]
        else:
            src, dst = landed.at[d, t - 1, m], landed.at[d, t, m]
        return pltpu.make_async_remote_copy(
            src_ref=src,
            dst_ref=dst,
            send_sem=zs.at[d, t, m],
            recv_sem=zr.at[d, t, m],
            device_id={"dp": right if d == 0 else left},
            device_id_type=MESH,
        )

    def sum_add(t, m, d):
        c = z + steps - t if d == 0 else z - steps + t
        if t == 1:
            mine, other = pl.ds(d * half, half), pl.ds((1 - d) * half, half)
            landed[d, 0, m, mine] = (
                landed[d, 0, m, mine].astype(F32) + parts[m, rows_of(c, d)].astype(F32)
            ).astype(BF)
            landed[d, 0, m, other] = parts[m, rows_of(c, 1 - d)]
        else:
            landed[d, t - 1, m] = (
                landed[d, t - 1, m].astype(F32) + parts[m, rows_of(c)].astype(F32)
            ).astype(BF)

    def spread_copy(t, m, d):
        c = z - t if d == 0 else z + t
        rows = rows_of(c, d) if t == steps - 1 else rows_of(c)
        return pltpu.make_async_remote_copy(
            src_ref=acts.at[m, rows],
            dst_ref=acts.at[m, rows],
            send_sem=gs.at[d, t, m],
            recv_sem=gr.at[d, t, m],
            device_id={"dp": right if d == 0 else left},
            device_id_type=MESH,
        )

    in_flight = ([], [])

    def launch(copy, d):
        if len(in_flight[d]) == DEPTH:
            in_flight[d].pop(0).wait_send()
        copy.start()
        in_flight[d].append(copy)

    def out_copy(i):
        peer = lax.rem(me + STRIDE * i, count)
        return pltpu.make_async_remote_copy(
            src_ref=source.at[part_of(peer)],
            dst_ref=held.at[me],
            send_sem=xs.at[i],
            recv_sem=xr.at[i],
            device_id={"expert": peer},
            device_id_type=MESH,
        )

    def back_copy(i):
        peer = lax.rem(me + STRIDE * i, count)
        return pltpu.make_async_remote_copy(
            src_ref=staged.at[peer],
            dst_ref=result.at[part_of(me)],
            send_sem=ys.at[i],
            recv_sem=yr.at[i],
            device_id={"expert": peer},
            device_id_type=MESH,
        )

    sides = (0, 1)
    for m in range(3):
        for d in sides:
            launch(sum_copy(0, m, d), d)
    own_out = pltpu.make_async_copy(source.at[part_of(me)], held.at[me], local.at[0])
    own_out.start()
    each(count, 1, lambda i: out_copy(i).start())

    for t in range(1, steps):
        for m in range(3):
            for d in sides:
                sum_copy(t - 1, m, d).wait_recv()
                sum_add(t, m, d)
                launch(sum_copy(t, m, d), d)

    def total(m):
        for d in sides:
            sum_copy(steps - 1, m, d).wait_recv()
        return (
            landed[0, steps - 1, m].astype(F32)
            + landed[1, steps - 1, m].astype(F32)
            + parts[m, rows_of(z)].astype(F32)
        )

    def spread_first(m, value):
        acts[m, rows_of(z)] = value.astype(BF)
        for d in sides:
            launch(spread_copy(0, m, d), d)

    gate = total(0)
    up = total(1)
    q = jax.nn.sigmoid(gate)
    silu = gate * q
    spread_first(2, silu * up)
    grad = total(2)
    spread_first(0, grad * up * q * (1.0 + gate * (1.0 - q)))
    spread_first(1, grad * silu)

    own_out.wait()
    each(count, 1, lambda i: out_copy(i).wait())
    own_back = pltpu.make_async_copy(staged.at[me], result.at[part_of(me)], local.at[1])
    if summing:
        run[0] = held[ints[0, 0]].astype(F32)

        def add(r):
            run[r] = run[r - 1] * flts[0, r] + held[ints[0, r]].astype(F32)

        each(count, 1, add)

    def fill(s):
        if summing:
            staged[s] = (run[ints[1, s]] * flts[1, s]).astype(BF)
        else:
            staged[s] = held[ints[0, s]]

    def fill_and_send(i):
        fill(lax.rem(me + STRIDE * i, count))
        back_copy(i).start()

    fill(me)
    own_back.start()
    each(count, 1, fill_and_send)

    for t in range(1, steps):
        for m in (2, 0, 1):
            for d in sides:
                spread_copy(t - 1, m, d).wait_recv()
                launch(spread_copy(t, m, d), d)
    for m in (2, 0, 1):
        for d in sides:
            spread_copy(steps - 1, m, d).wait_recv()
    for d in sides:
        for copy in in_flight[d]:
            copy.wait_send()
    own_back.wait()
    each(count, 1, lambda i: back_copy(i).wait())


def stage(parts, source, ints, flts, summing, ring, collective_id):
    count = ints.shape[1]
    rows, width = source.shape
    row_blocks = 8
    source = source.reshape(row_blocks, rows // row_blocks, width)
    piece = (count, rows // row_blocks, width * row_blocks // count)
    steps = ring // 2
    chunk = parts.shape[1] // ring
    sem = pltpu.SemaphoreType.DMA
    acts, result = pl.pallas_call(
        functools.partial(stage_kernel, summing, count, ring),
        out_shape=(
            jax.ShapeDtypeStruct(parts.shape, BF),
            jax.ShapeDtypeStruct(source.shape, BF),
        ),
        in_specs=[pl.BlockSpec(memory_space=pltpu.SMEM)] * 2
        + [pl.BlockSpec(memory_space=VMEM)] * 2,
        out_specs=[pl.BlockSpec(memory_space=VMEM)] * 2,
        scratch_shapes=[
            VMEM((2, steps, 3, chunk, parts.shape[2]), BF),
            VMEM(piece, BF),
            VMEM(piece, BF),
            VMEM(piece if summing else (1, 8, 128), F32),
            sem((2, steps, 3)),
            sem((2, steps, 3)),
            sem((2, steps, 3)),
            sem((2, steps, 3)),
            sem((count,)),
            sem((count,)),
            sem((count,)),
            sem((count,)),
            sem((2,)),
        ],
        compiler_params=pltpu.CompilerParams(
            collective_id=collective_id, has_side_effects=True, vmem_limit_bytes=40 << 20
        ),
        name=f"stage{collective_id}",
    )(ints, flts, parts, source)
    return acts, result.reshape(rows, width)


def body(tokens, cotangent, slot_ids, gates, plan, w_gate, w_up, w_down):
    count = lax.axis_size("expert")
    ring = lax.axis_size("dp")
    token_count, width = tokens.shape
    choose = slot_ids.shape[1]
    hidden = w_gate.shape[2]
    slots = 2 * count
    capacity = 5 * token_count * choose // (4 * slots)
    pair = 2 * capacity
    columns = count * pair
    rows = count * capacity
    half = hidden // 2

    named = slot_ids[:, :, None] == jnp.arange(slots, dtype=jnp.int32)
    names = jnp.sum(named.astype(F32), axis=1)
    t_ids = jnp.arange(token_count, dtype=jnp.int32)
    before = (t_ids[:, None] > t_ids[None, :]).astype(BF)
    turns = jnp.dot(before, names.astype(BF), preferred_element_type=F32)
    turn = jnp.sum(jnp.where(named, turns[:, None, :], 0.0), axis=2).astype(jnp.int32)
    place = (slot_ids % count) * pair + (slot_ids // count) * capacity + turn
    column_ids = jnp.arange(columns, dtype=jnp.int32)
    hits = place[:, :, None] == column_ids
    chosen = jnp.sum(hits.astype(F32), axis=1).astype(BF)
    weight = jnp.sum(jnp.where(hits, gates[:, :, None], 0.0), axis=1)
    gate_of = jnp.sum(weight, axis=0)

    both = jnp.concatenate([tokens, cotangent], axis=1)
    picked = lax.dot_general(chosen, both, (((0,), (0,)), ((), ())), preferred_element_type=F32)
    scale = jnp.where(jnp.arange(2 * width)[None, :] < width, 1.0, gate_of[:, None])
    sent = (picked * scale).astype(BF).reshape(count, pair, 2 * width)
    got = exchange(sent, 1).reshape(columns, 2 * width)

    r_ids = jnp.arange(columns, dtype=jnp.int32)
    target = (r_ids % pair) // capacity * rows + r_ids // pair * capacity + r_ids % capacity
    sort = (target[:, None] == column_ids[None, :]).astype(BF)
    features = lax.dot_general(
        got, sort, (((0,), (0,)), ((), ())), preferred_element_type=F32
    ).astype(BF)
    inputs = []
    for k in range(2):
        x = features[:width, k * rows : (k + 1) * rows]
        zz = features[width:, k * rows : (k + 1) * rows]
        inputs.append(jnp.stack([x, x, zz]))

    down_t = jnp.swapaxes(w_down[0], 0, 1)
    home = [
        jnp.stack([w[:, h * half : (h + 1) * half] for w in (w_gate[0], w_up[0], down_t)])
        for h in range(2)
    ]
    flat = 3 * width

    s_ids = jnp.arange(count, dtype=jnp.int32)
    ahead = (plan[None, :] < plan[:, None]) | (
        (plan[None, :] == plan[:, None]) & (s_ids[None, :] < s_ids[:, None])
    )
    rank = jnp.sum(ahead.astype(jnp.int32), axis=1)
    at_rank = rank[None, :] == s_ids[:, None]
    order = jnp.sum(jnp.where(at_rank, s_ids[None, :], 0), axis=1)
    expert_at = jnp.sum(jnp.where(at_rank, plan[None, :], 0), axis=1)
    same = jnp.sum(
        jnp.where(s_ids[None, :] == s_ids[:, None] - 1, expert_at[None, :], 0), axis=1
    )
    keep = ((same == expert_at) & (s_ids > 0)).astype(F32)
    upto = jnp.sum((plan[None, :] <= s_ids[:, None]).astype(jnp.int32), axis=1)
    some = jnp.any(plan[None, :] == s_ids[:, None], axis=1).astype(F32)
    sum_ints = jnp.stack([order, jnp.maximum(upto - 1, 0)])
    sum_flts = jnp.stack([keep, some])
    pick_ints = plan[None, :]
    pick_flts = jnp.zeros((1, count), F32)

    def products(weights, k):
        return jnp.einsum(
            "mfh,mfr->mhr", weights, inputs[k], preferred_element_type=F32
        ).astype(BF)

    def slot_grads(acts, k):
        return jnp.einsum("mfr,mhr->mfh", inputs[k], acts, preferred_element_type=F32)

    def slot_rows(weights, acts):
        back = jnp.dot(weights[0], acts[0], preferred_element_type=F32) + jnp.dot(
            weights[1], acts[1], preferred_element_type=F32
        )
        return back, jnp.dot(weights[2], acts[2], preferred_element_type=F32)

    home_acts0, replica0 = stage(
        products(home[0], 0), home[0].reshape(flat, half), pick_ints, pick_flts, False, ring, 2
    )
    replica0 = replica0.reshape(3, width, half)
    rep_acts0, replica1 = stage(
        products(replica0, 1), home[1].reshape(flat, half), pick_ints, pick_flts, False, ring, 3
    )
    replica1 = replica1.reshape(3, width, half)
    rep_grads0 = slot_grads(rep_acts0, 1).astype(BF).reshape(flat, half)
    rep_acts1, summed0 = stage(
        products(replica1, 1), rep_grads0, sum_ints, sum_flts, True, ring, 4
    )
    rep_grads1 = slot_grads(rep_acts1, 1).astype(BF).reshape(flat, half)
    home_acts1, summed1 = stage(
        products(home[1], 0), rep_grads1, sum_ints, sum_flts, True, ring, 5
    )

    made = []
    for weights, acts in (
        ((home[0], home[1]), (home_acts0, home_acts1)),
        ((replica0, replica1), (rep_acts0, rep_acts1)),
    ):
        back0, out0 = slot_rows(weights[0], acts[0])
        back1, out1 = slot_rows(weights[1], acts[1])
        made.append(jnp.concatenate([out0 + out1, back0 + back1]).astype(BF))
    made = jnp.concatenate(made, axis=1)
    returned = exchange(
        lax.dot_general(sort, made, (((1,), (1,)), ((), ())), preferred_element_type=F32)
        .astype(BF)
        .reshape(count, pair, 2 * width),
        6,
    ).reshape(columns, 2 * width)
    high = weight.astype(BF)
    low = (weight - high.astype(F32)).astype(BF)
    output = (
        jnp.dot(high, returned[:, :width], preferred_element_type=F32)
        + jnp.dot(low, returned[:, :width], preferred_element_type=F32)
    ).astype(BF)
    token_grad = jnp.dot(chosen, returned[:, width:], preferred_element_type=F32).astype(BF)

    home_grads = [slot_grads(home_acts0, 0), slot_grads(home_acts1, 0)]
    summed = [summed0.reshape(3, width, half), summed1.reshape(3, width, half)]
    grads = [
        jnp.concatenate([home_grads[h][m] + summed[h][m].astype(F32) for h in range(2)], axis=1)
        for m in range(3)
    ]
    return (
        output,
        token_grad,
        grads[0][None],
        grads[1][None],
        jnp.swapaxes(grads[2], 0, 1)[None],
    )


def solution(mesh):
    in_specs = (
        P("expert", "dp"),
        P("expert", "dp"),
        P("expert", None),
        P("expert", None),
        P(),
        P("expert", "dp", None),
        P("expert", "dp", None),
        P("expert", None, "dp"),
    )
    out_specs = (
        P("expert", "dp"),
        P("expert", "dp"),
        P("expert", "dp", None),
        P("expert", "dp", None),
        P("expert", None, "dp"),
    )
    return jax.shard_map(body, mesh=mesh, in_specs=in_specs, out_specs=out_specs, check_vma=False)
```

```python
import functools

import jax
import jax.numpy as jnp
from jax import lax
from jax.experimental import pallas as pl
from jax.experimental.pallas import tpu as pltpu
from jax.sharding import PartitionSpec as P

MESH = pl.DeviceIdType.MESH
BF = jnp.bfloat16
F32 = jnp.float32
VMEM = pltpu.VMEM
DEPTH = 2
STRIDE = 11


def greet(axis, peers):
    barrier = pltpu.get_barrier_semaphore()
    for peer in peers:
        pl.semaphore_signal(barrier, inc=1, device_id={axis: peer}, device_id_type=MESH)


def greet_all(axis, count, me):
    barrier = pltpu.get_barrier_semaphore()

    def one(i, carry):
        pl.semaphore_signal(
            barrier, inc=1, device_id={axis: lax.rem(me + i, count)}, device_id_type=MESH
        )
        return carry

    lax.fori_loop(1, count, one, 0)


def each(count, first, function):
    def step(i, carry):
        function(i)
        return carry

    lax.fori_loop(first, count, step, 0)


def matmul(a, b, ca, cb):
    return lax.dot_general(a, b, (((ca,), (cb,)), ((), ())), preferred_element_type=F32)


def layer_kernel(
    count, ring, capacity, ints, flts, sent, weights,
    returned, grads,
    got, home_acts, summed, xs_ref, zs_ref, copied, parts, rep_acts, landed, held_even, held_odd, staged, run, slot_grads, rows_acc, made,
    z_send, z_recv, g_send, g_recv, out_send, out_recv, back_send, back_recv, ex_send, ex_recv, local,
):
    me = lax.axis_index("expert")
    z = lax.axis_index("dp")
    right, left = lax.rem(z + 1, ring), lax.rem(z + ring - 1, ring)
    width, rows = xs_ref.shape[1], xs_ref.shape[2]
    half_hidden = parts.shape[2]
    chunk = half_hidden // ring
    half = chunk // 2
    steps = ring // 2
    pair = 2 * capacity
    row_blocks = 8
    lane_blocks = count // row_blocks
    piece_rows, piece = held_even.shape[1], held_even.shape[2]
    sides = (0, 1)

    greet("dp", (right, left))
    greet_all("expert", count, me)
    pl.semaphore_wait(pltpu.get_barrier_semaphore(), count + 1)

    def peer_of(i):
        return lax.rem(me + STRIDE * i, count)

    def to_peer(src, dst, send, recv, peer):
        return pltpu.make_async_remote_copy(
            src_ref=src, dst_ref=dst, send_sem=send, recv_sem=recv,
            device_id={"expert": peer}, device_id_type=MESH,
        )

    def exchange(src, dst, turn):
        def copy(i):
            peer = peer_of(i)
            return to_peer(
                src.at[peer], dst.at[me], ex_send.at[turn, i], ex_recv.at[turn, i], peer
            )

        own = pltpu.make_async_copy(src.at[me], dst.at[me], local.at[2 + turn])
        own.start()
        each(count, 1, lambda i: copy(i).start())

        def finish():
            own.wait()
            each(count, 1, lambda i: copy(i).wait())

        return finish

    def part_of(block):
        row = pl.multiple_of(lax.div(block, lane_blocks) * piece_rows, 16)
        lane = pl.multiple_of(lax.rem(block, lane_blocks) * piece, piece)
        return (pl.ds(row, piece_rows), pl.ds(lane, piece))

    class Move:
        def __init__(self, turn, source, result, summing):
            self.p, self.source, self.result, self.summing = turn % 2, source, result, summing
            self.held = held_odd if self.p else held_even

        def out_copy(self, i):
            peer = peer_of(i)
            return to_peer(
                self.source.at[part_of(peer)], self.held.at[me],
                out_send.at[self.p, i], out_recv.at[self.p, i], peer,
            )

        def back_copy(self, i):
            peer = peer_of(i)
            return to_peer(
                staged.at[self.p, peer], self.result.at[part_of(me)],
                back_send.at[self.p, i], back_recv.at[self.p, i], peer,
            )

        def own_out(self):
            return pltpu.make_async_copy(
                self.source.at[part_of(me)], self.held.at[me], local.at[0]
            )

        def own_back(self):
            return pltpu.make_async_copy(
                staged.at[self.p, me], self.result.at[part_of(me)], local.at[1]
            )

        def begin(self):
            self.own_out().start()
            each(count, 1, lambda i: self.out_copy(i).start())

        def pass_on(self):
            self.own_out().wait()
            each(count, 1, lambda i: self.out_copy(i).wait())
            if self.summing:
                run[0] = self.held[0].astype(F32)

                def add(r):
                    run[r] = run[ints[1, r]] * flts[0, r] + self.held[r].astype(F32)

                each(count, 1, add)

            def fill(i):
                s = peer_of(i)
                if self.summing:
                    staged[self.p, s] = (run[ints[2, s]] * flts[1, s]).astype(BF)
                else:
                    staged[self.p, s] = self.held[ints[0, s]]

            fill(0)
            self.own_back().start()

            def fill_and_send(i):
                fill(i)
                self.back_copy(i).start()

            each(count, 1, fill_and_send)

        def finish(self):
            self.own_back().wait()
            each(count, 1, lambda i: self.back_copy(i).wait())

    def multiply_parts(w, k, p):
        def for_input(m, src):
            def tile(b):
                lane = pl.ds(pl.multiple_of(b * 128, 128), 128)
                parts[p, m, lane] = matmul(
                    w[pl.ds(m * width, width), lane], src[k], 0, 0
                ).astype(BF)

            each(half_hidden // 128, 0, tile)

        for m in range(3):
            for_input(m, zs_ref if m == 2 else xs_ref)

    tile_rows = width // 4

    def multiply_grads(acts, k, dst):
        for m in range(3):
            src = zs_ref if m == 2 else xs_ref

            def tile(b, m=m, src=src):
                row = pl.multiple_of(b * tile_rows, tile_rows)
                dst[pl.ds(m * width + row, tile_rows)] = matmul(
                    src[k, pl.ds(row, tile_rows)], acts[m], 1, 1
                ).astype(BF)

            each(4, 0, tile)

    def home_grads(h):
        lane = pl.ds(h * half_hidden, half_hidden)
        for m in range(3):
            src = zs_ref if m == 2 else xs_ref

            def tile(b, m=m, src=src):
                row = pl.multiple_of(b * tile_rows, tile_rows)
                at = pl.ds(m * width + row, tile_rows)
                grads[at, lane] = matmul(
                    src[0, pl.ds(row, tile_rows)], home_acts[h, m], 1, 1
                ) + summed[h, at].astype(F32)

            each(4, 0, tile)

    def multiply_rows(w, acts, store):
        def tile(b):
            row = pl.multiple_of(b * tile_rows, tile_rows)
            down = pl.ds(2 * width + row, tile_rows)
            store(row, matmul(w[down], acts[2], 1, 0))
            up = pl.ds(width + row, tile_rows)
            store(
                width + row,
                matmul(w[pl.ds(row, tile_rows)], acts[0], 1, 0)
                + matmul(w[up], acts[1], 1, 0),
            )

        each(4, 0, tile)

    def keep_rows(k):
        def store(row, value):
            rows_acc[k, pl.ds(row, tile_rows)] = value

        return store

    def end_rows(k):
        def store(row, value):
            at = pl.ds(row, tile_rows)
            made[k, at] = (rows_acc[k, at] + value).astype(BF)

        return store

    def sort_rows():
        sources = 8
        for n in range(rows // 128):
            first = min(128 * n // capacity, count - sources)
            block = got[pl.ds(first, sources)].reshape(sources * pair, 2 * width)
            shape = (sources * pair, 128)
            r = lax.broadcasted_iota(jnp.int32, shape, 0)
            lane = lax.broadcasted_iota(jnp.int32, shape, 1) + 128 * n
            inside = lax.rem(r, pair)
            goes_to = (lax.div(r, pair) + first) * capacity + lax.rem(inside, capacity)
            for k in range(2):
                hit = (goes_to == lane) & (lax.div(inside, capacity) == k)
                tile = matmul(block, jnp.where(hit, 1.0, 0.0).astype(BF), 0, 0)
                at = pl.ds(128 * n, 128)
                xs_ref[k, :, at] = tile[:width].astype(BF)
                zs_ref[k, :, at] = tile[width:].astype(BF)

    def unsort_rows(k, first):
        sources, window = 4, 256
        blocks = count // sources

        def block(b):
            start = lax.min(lax.div(b * sources * capacity, 128) * 128, rows - window)
            start = pl.multiple_of(start, 128)
            shape = (sources * pair, window)
            r = lax.broadcasted_iota(jnp.int32, shape, 0)
            lane = lax.broadcasted_iota(jnp.int32, shape, 1) + start
            inside = lax.rem(r, pair)
            comes_from = (lax.div(r, pair) + b * sources) * capacity + lax.rem(inside, capacity)
            hit = (comes_from == lane) & (lax.div(inside, capacity) == k)
            tile = matmul(
                jnp.where(hit, 1.0, 0.0).astype(BF), made[k, :, pl.ds(start, window)], 1, 1
            ).reshape(sources, pair, 2 * width)
            at = pl.ds(b * sources, sources)
            if first:
                got[at] = tile.astype(BF)
            else:
                got[at] = (got[at].astype(F32) + tile).astype(BF)

        each(blocks, 0, block)

    def over_dp(p, acts, early, middle, late):
        def rows_of(c, d=None):
            base = lax.rem(c + 2 * ring, ring) * chunk
            if d is None:
                return pl.ds(pl.multiple_of(base, chunk), chunk)
            return pl.ds(pl.multiple_of(base + d * half, half), half)

        def sum_copy(t, m, d):
            c = z + steps - t if d == 0 else z - steps + t
            if t == 0:
                src = parts.at[p, m, rows_of(c, d)]
                dst = landed.at[p, d, 0, m, pl.ds(d * half, half)]
            else:
                src, dst = landed.at[p, d, t - 1, m], landed.at[p, d, t, m]
            return pltpu.make_async_remote_copy(
                src_ref=src,
                dst_ref=dst,
                send_sem=z_send.at[p, d, t, m],
                recv_sem=z_recv.at[p, d, t, m],
                device_id={"dp": right if d == 0 else left},
                device_id_type=MESH,
            )

        def sum_add(t, m, d):
            c = z + steps - t if d == 0 else z - steps + t
            if t == 1:
                mine, other = pl.ds(d * half, half), pl.ds((1 - d) * half, half)
                landed[p, d, 0, m, mine] = (
                    landed[p, d, 0, m, mine].astype(F32) + parts[p, m, rows_of(c, d)].astype(F32)
                ).astype(BF)
                landed[p, d, 0, m, other] = parts[p, m, rows_of(c, 1 - d)]
            else:
                landed[p, d, t - 1, m] = (
                    landed[p, d, t - 1, m].astype(F32) + parts[p, m, rows_of(c)].astype(F32)
                ).astype(BF)

        def spread_copy(t, m, d):
            c = z - t if d == 0 else z + t
            at = rows_of(c, d) if t == steps - 1 else rows_of(c)
            return pltpu.make_async_remote_copy(
                src_ref=acts.at[m, at],
                dst_ref=acts.at[m, at],
                send_sem=g_send.at[p, d, t, m],
                recv_sem=g_recv.at[p, d, t, m],
                device_id={"dp": right if d == 0 else left},
                device_id_type=MESH,
            )

        in_flight = ([], [])

        def launch(copy, d):
            if len(in_flight[d]) == DEPTH:
                in_flight[d].pop(0).wait_send()
            copy.start()
            in_flight[d].append(copy)

        for m in range(3):
            for d in sides:
                launch(sum_copy(0, m, d), d)
        early()
        for t in range(1, steps):
            for m in range(3):
                for d in sides:
                    sum_copy(t - 1, m, d).wait_recv()
                    sum_add(t, m, d)
                    launch(sum_copy(t, m, d), d)

        def total(m):
            for d in sides:
                sum_copy(steps - 1, m, d).wait_recv()
            return (
                landed[p, 0, steps - 1, m].astype(F32)
                + landed[p, 1, steps - 1, m].astype(F32)
                + parts[p, m, rows_of(z)].astype(F32)
            )

        def spread_first(m, value):
            acts[m, rows_of(z)] = value.astype(BF)
            for d in sides:
                launch(spread_copy(0, m, d), d)

        gate = total(0)
        up = total(1)
        q = jax.nn.sigmoid(gate)
        silu = gate * q
        spread_first(2, silu * up)
        grad = total(2)
        spread_first(0, grad * up * q * (1.0 + gate * (1.0 - q)))
        spread_first(1, grad * silu)
        middle()
        for t in range(1, steps):
            for m in (2, 0, 1):
                for d in sides:
                    spread_copy(t - 1, m, d).wait_recv()
                    launch(spread_copy(t, m, d), d)
            if t == 1:
                late()
        for m in (2, 0, 1):
            for d in sides:
                spread_copy(steps - 1, m, d).wait_recv()
        for d in sides:
            for copy in in_flight[d]:
                copy.wait_send()

    def nothing():
        pass

    moves = [
        Move(0, weights.at[0], copied.at[0], False),
        Move(1, weights.at[1], copied.at[1], False),
        Move(2, slot_grads.at[0], summed.at[0], True),
        Move(3, slot_grads.at[1], summed.at[1], True),
    ]
    pad = slot_grads.shape[1] - 3 * width
    if pad:
        for h in range(2):
            slot_grads[h, pl.ds(3 * width, pad)] = jnp.zeros((pad, half_hidden), BF)
    exchange(sent, got, 0)()
    moves[0].begin()
    sort_rows()
    multiply_parts(weights.at[0], 0, 0)
    over_dp(0, home_acts.at[0], nothing, moves[0].pass_on, nothing)
    moves[0].finish()
    moves[1].begin()
    multiply_parts(copied.at[0], 1, 1)
    over_dp(
        1,
        rep_acts.at[0],
        lambda: multiply_rows(weights.at[0], home_acts.at[0], keep_rows(0)),
        moves[1].pass_on,
        nothing,
    )
    moves[1].finish()
    multiply_parts(copied.at[1], 1, 0)

    def first_grads():
        multiply_grads(rep_acts.at[0], 1, slot_grads.at[0])
        moves[2].begin()
        multiply_rows(copied.at[0], rep_acts.at[0], keep_rows(1))

    over_dp(0, rep_acts.at[1], first_grads, moves[2].pass_on, nothing)
    multiply_parts(weights.at[1], 0, 1)
    moves[2].finish()

    def second_grads():
        multiply_grads(rep_acts.at[1], 1, slot_grads.at[1])
        moves[3].begin()

    def replica_rows():
        multiply_rows(copied.at[1], rep_acts.at[1], end_rows(1))
        unsort_rows(1, True)

    over_dp(1, home_acts.at[1], second_grads, moves[3].pass_on, replica_rows)
    multiply_rows(weights.at[1], home_acts.at[1], end_rows(0))
    unsort_rows(0, False)
    done = exchange(got, returned, 1)
    home_grads(0)
    moves[3].finish()
    home_grads(1)
    done()


def layer(sent, weights, ints, flts, capacity, ring):
    count, pair, two_width = sent.shape
    width = two_width // 2
    flat, half_hidden = weights.shape[1:]
    rows = count * capacity
    steps = ring // 2
    chunk = half_hidden // ring
    piece = (flat // 8, half_hidden * 8 // count)
    sem = pltpu.SemaphoreType.DMA
    acts = (2, 3, half_hidden, rows)
    return pl.pallas_call(
        functools.partial(layer_kernel, count, ring, capacity),
        out_shape=(
            jax.ShapeDtypeStruct(sent.shape, BF),
            jax.ShapeDtypeStruct((3 * width, 2 * half_hidden), F32),
        ),
        in_specs=[pl.BlockSpec(memory_space=pltpu.SMEM)] * 2
        + [pl.BlockSpec(memory_space=VMEM)] * 2,
        out_specs=[pl.BlockSpec(memory_space=VMEM)] * 2,
        scratch_shapes=[
            VMEM(sent.shape, BF),
            VMEM(acts, BF),
            VMEM(weights.shape, BF),
            VMEM((2, width, rows), BF),
            VMEM((2, width, rows), BF),
            VMEM(weights.shape, BF),
            VMEM((2, 3, half_hidden, rows), BF),
            VMEM(acts, BF),
            VMEM((2, 2, steps, 3, chunk, rows), BF),
            VMEM((count,) + piece, BF),
            VMEM((count,) + piece, BF),
            VMEM((2, count) + piece, BF),
            VMEM((count,) + piece, F32),
            VMEM(weights.shape, BF),
            VMEM((2, two_width, rows), F32),
            VMEM((2, two_width, rows), BF),
            sem((2, 2, steps, 3)),
            sem((2, 2, steps, 3)),
            sem((2, 2, steps, 3)),
            sem((2, 2, steps, 3)),
            sem((2, count)),
            sem((2, count)),
            sem((2, count)),
            sem((2, count)),
            sem((2, count)),
            sem((2, count)),
            sem((4,)),
        ],
        compiler_params=pltpu.CompilerParams(
            collective_id=1, has_side_effects=True, vmem_limit_bytes=62 << 20
        ),
        name="layer",
    )(ints, flts, sent, weights)


def body(tokens, cotangent, slot_ids, gates, plan, w_gate, w_up, w_down):
    count = lax.axis_size("expert")
    ring = lax.axis_size("dp")
    token_count, width = tokens.shape
    choose = slot_ids.shape[1]
    hidden = w_gate.shape[2]
    slots = 2 * count
    capacity = 5 * token_count * choose // (4 * slots)
    pair = 2 * capacity
    columns = count * pair
    rows = count * capacity
    half = hidden // 2

    named = slot_ids[:, :, None] == jnp.arange(slots, dtype=jnp.int32)
    names = jnp.sum(named.astype(F32), axis=1)
    t_ids = jnp.arange(token_count, dtype=jnp.int32)
    before = (t_ids[:, None] > t_ids[None, :]).astype(BF)
    turns = jnp.dot(before, names.astype(BF), preferred_element_type=F32)
    turn = jnp.sum(jnp.where(named, turns[:, None, :], 0.0), axis=2).astype(jnp.int32)
    place = (slot_ids % count) * pair + (slot_ids // count) * capacity + turn
    column_ids = jnp.arange(columns, dtype=jnp.int32)
    hits = place[:, :, None] == column_ids
    chosen = jnp.sum(hits.astype(F32), axis=1).astype(BF)
    weight = jnp.sum(jnp.where(hits, gates[:, :, None], 0.0), axis=1)
    gate_of = jnp.sum(weight, axis=0)

    both = jnp.concatenate([tokens, cotangent], axis=1)
    picked = lax.dot_general(chosen, both, (((0,), (0,)), ((), ())), preferred_element_type=F32)
    scale = jnp.where(jnp.arange(2 * width)[None, :] < width, 1.0, gate_of[:, None])
    sent = (picked * scale).astype(BF).reshape(count, pair, 2 * width)
    down_t = jnp.swapaxes(w_down[0], 0, 1)
    flat = -(-3 * width // (8 * 16)) * 8 * 16
    filler = jnp.zeros((flat - 3 * width, hidden), BF)
    whole = jnp.concatenate([w_gate[0], w_up[0], down_t, filler])
    weights = jnp.stack([whole[:, h * half : (h + 1) * half] for h in range(2)])

    s_ids = jnp.arange(count, dtype=jnp.int32)
    sought = jnp.concatenate([plan, s_ids])
    limit = jnp.concatenate([s_ids, jnp.full((count,), count, jnp.int32)])
    match = (plan[None, :] == sought[:, None]) & (s_ids[None, :] < limit[:, None])
    found = jnp.max(jnp.where(match, s_ids[None, :], -1), axis=1)
    ints = jnp.concatenate([plan, jnp.maximum(found, 0)]).reshape(3, count)
    flts = (found >= 0).astype(F32).reshape(2, count)

    returned, grads = layer(sent, weights, ints, flts, capacity, ring)
    returned = returned.reshape(columns, 2 * width)
    high = weight.astype(BF)
    low = (weight - high.astype(F32)).astype(BF)
    output = (
        jnp.dot(high, returned[:, :width], preferred_element_type=F32)
        + jnp.dot(low, returned[:, :width], preferred_element_type=F32)
    ).astype(BF)
    token_grad = jnp.dot(chosen, returned[:, width:], preferred_element_type=F32).astype(BF)

    return (
        output,
        token_grad,
        grads[:width][None],
        grads[width : 2 * width][None],
        jnp.swapaxes(grads[2 * width :], 0, 1)[None],
    )


def solution(mesh):
    in_specs = (
        P("expert", "dp"),
        P("expert", "dp"),
        P("expert", None),
        P("expert", None),
        P(),
        P("expert", "dp", None),
        P("expert", "dp", None),
        P("expert", None, "dp"),
    )
    out_specs = (
        P("expert", "dp"),
        P("expert", "dp"),
        P("expert", "dp", None),
        P("expert", "dp", None),
        P("expert", None, "dp"),
    )
    return jax.shard_map(body, mesh=mesh, in_specs=in_specs, out_specs=out_specs, check_vma=False)
```

```python
import functools

import jax
import jax.numpy as jnp
from jax import lax
from jax.experimental import pallas as pl
from jax.experimental.pallas import tpu as pltpu
from jax.sharding import PartitionSpec as P

MESH = pl.DeviceIdType.MESH
BF = jnp.bfloat16
F32 = jnp.float32
VMEM = pltpu.VMEM
DEPTH = 2
STRIDE = 11


def greet(axis, peers):
    barrier = pltpu.get_barrier_semaphore()
    for peer in peers:
        pl.semaphore_signal(barrier, inc=1, device_id={axis: peer}, device_id_type=MESH)


def greet_all(axis, count, me):
    barrier = pltpu.get_barrier_semaphore()

    def one(i, carry):
        pl.semaphore_signal(
            barrier, inc=1, device_id={axis: lax.rem(me + i, count)}, device_id_type=MESH
        )
        return carry

    lax.fori_loop(1, count, one, 0)


def each(count, first, function):
    def step(i, carry):
        function(i)
        return carry

    lax.fori_loop(first, count, step, 0)


def matmul(a, b, ca, cb):
    return lax.dot_general(a, b, (((ca,), (cb,)), ((), ())), preferred_element_type=F32)


def layer_kernel(
    count, ring, capacity, plan, before_it, last_of, ids, gates, both, w_gate, w_up, w_down,
    results, grads,
    weights, sent, returned, chosen, high, low, got, home_acts, summed, xs_ref, zs_ref, copied, parts, rep_acts, landed, held_even, held_odd, staged, run, slot_grads, rows_acc, made,
    z_send, z_recv, g_send, g_recv, out_send, out_recv, back_send, back_recv, ex_send, ex_recv, local, placed,
):
    me = lax.axis_index("expert")
    z = lax.axis_index("dp")
    right, left = lax.rem(z + 1, ring), lax.rem(z + ring - 1, ring)
    width, rows = xs_ref.shape[1], xs_ref.shape[2]
    half_hidden = parts.shape[2]
    chunk = half_hidden // ring
    half = chunk // 2
    steps = ring // 2
    pair = 2 * capacity
    row_blocks = 8
    lane_blocks = count // row_blocks
    piece_rows, piece = held_even.shape[1], held_even.shape[2]
    sides = (0, 1)

    def place_copy(h, m):
        lane = pl.ds(h * half_hidden, half_hidden)
        return pltpu.make_async_copy(
            (w_gate, w_up, w_down)[m].at[:, lane],
            weights.at[h, pl.ds(m * width, width)],
            placed.at[h, m],
        )

    for h in range(2):
        for m in range(3):
            place_copy(h, m).start()
    greet("dp", (right, left))
    greet_all("expert", count, me)
    pad = weights.shape[1] - 3 * width
    if pad:
        for h in range(2):
            for ref in (weights, slot_grads):
                ref[h, pl.ds(3 * width, pad)] = jnp.zeros((pad, half_hidden), BF)
    pl.semaphore_wait(pltpu.get_barrier_semaphore(), count + 1)

    def peer_of(i):
        return lax.rem(me + STRIDE * i, count)

    def to_peer(src, dst, send, recv, peer):
        return pltpu.make_async_remote_copy(
            src_ref=src, dst_ref=dst, send_sem=send, recv_sem=recv,
            device_id={"expert": peer}, device_id_type=MESH,
        )

    def exchange(src, dst, turn):
        def copy(i):
            peer = peer_of(i)
            return to_peer(
                src.at[peer], dst.at[me], ex_send.at[turn, i], ex_recv.at[turn, i], peer
            )

        own = pltpu.make_async_copy(src.at[me], dst.at[me], local.at[2 + turn])
        own.start()
        each(count, 1, lambda i: copy(i).start())

        def finish():
            own.wait()
            each(count, 1, lambda i: copy(i).wait())

        return finish

    def part_of(block):
        row = pl.multiple_of(lax.div(block, lane_blocks) * piece_rows, 16)
        lane = pl.multiple_of(lax.rem(block, lane_blocks) * piece, piece)
        return (pl.ds(row, piece_rows), pl.ds(lane, piece))

    class Move:
        def __init__(self, turn, source, result, summing):
            self.p, self.source, self.result, self.summing = turn % 2, source, result, summing
            self.held = held_odd if self.p else held_even

        def out_copy(self, i):
            peer = peer_of(i)
            return to_peer(
                self.source.at[part_of(peer)], self.held.at[me],
                out_send.at[self.p, i], out_recv.at[self.p, i], peer,
            )

        def back_copy(self, i):
            peer = peer_of(i)
            return to_peer(
                staged.at[self.p, peer], self.result.at[part_of(me)],
                back_send.at[self.p, i], back_recv.at[self.p, i], peer,
            )

        def own_out(self):
            return pltpu.make_async_copy(
                self.source.at[part_of(me)], self.held.at[me], local.at[0]
            )

        def own_back(self):
            return pltpu.make_async_copy(
                staged.at[self.p, me], self.result.at[part_of(me)], local.at[1]
            )

        def begin(self):
            self.own_out().start()
            each(count, 1, lambda i: self.out_copy(i).start())

        def pass_on(self):
            self.own_out().wait()
            each(count, 1, lambda i: self.out_copy(i).wait())
            if self.summing:
                run[0] = self.held[0].astype(F32)

                def add(r):
                    prior = before_it[r]
                    keep = jnp.where(prior >= 0, 1.0, 0.0)
                    run[r] = run[jnp.maximum(prior, 0)] * keep + self.held[r].astype(F32)

                each(count, 1, add)

            def fill(i):
                s = peer_of(i)
                if self.summing:
                    final = last_of[s]
                    some = jnp.where(final >= 0, 1.0, 0.0)
                    staged[self.p, s] = (run[jnp.maximum(final, 0)] * some).astype(BF)
                else:
                    staged[self.p, s] = self.held[plan[s]]

            fill(0)
            self.own_back().start()

            def fill_and_send(i):
                fill(i)
                self.back_copy(i).start()

            each(count, 1, fill_and_send)

        def finish(self):
            self.own_back().wait()
            each(count, 1, lambda i: self.back_copy(i).wait())

    def multiply_parts(w, k, p):
        def for_input(m, src):
            def tile(b):
                lane = pl.ds(pl.multiple_of(b * 128, 128), 128)
                parts[p, m, lane] = matmul(
                    w[pl.ds(m * width, width), lane], src[k], 0, 0
                ).astype(BF)

            each(half_hidden // 128, 0, tile)

        for m in range(3):
            for_input(m, zs_ref if m == 2 else xs_ref)

    tile_rows = width // 4

    def multiply_grads(acts, k, dst):
        for m in range(3):
            src = zs_ref if m == 2 else xs_ref

            def tile(b, m=m, src=src):
                row = pl.multiple_of(b * tile_rows, tile_rows)
                dst[pl.ds(m * width + row, tile_rows)] = matmul(
                    src[k, pl.ds(row, tile_rows)], acts[m], 1, 1
                ).astype(BF)

            each(4, 0, tile)

    def home_grads(h):
        lane = pl.ds(h * half_hidden, half_hidden)
        for m in range(3):
            src = zs_ref if m == 2 else xs_ref

            def tile(b, m=m, src=src):
                row = pl.multiple_of(b * tile_rows, tile_rows)
                at = pl.ds(m * width + row, tile_rows)
                grads[at, lane] = matmul(
                    src[0, pl.ds(row, tile_rows)], home_acts[h, m], 1, 1
                ) + summed[h, at].astype(F32)

            each(4, 0, tile)

    def multiply_rows(w, acts, store):
        def tile(b):
            row = pl.multiple_of(b * tile_rows, tile_rows)
            down = pl.ds(2 * width + row, tile_rows)
            store(row, matmul(w[down], acts[2], 1, 0))
            up = pl.ds(width + row, tile_rows)
            store(
                width + row,
                matmul(w[pl.ds(row, tile_rows)], acts[0], 1, 0)
                + matmul(w[up], acts[1], 1, 0),
            )

        each(4, 0, tile)

    def keep_rows(k):
        def store(row, value):
            rows_acc[k, pl.ds(row, tile_rows)] = value

        return store

    def end_rows(k):
        def store(row, value):
            at = pl.ds(row, tile_rows)
            made[k, at] = (rows_acc[k, at] + value).astype(BF)

        return store

    row_tiles = 2
    tile_columns = count * pair // row_tiles
    tile_sources = count // row_tiles

    def send_rows():
        tokens, choose = ids.shape
        slot = lax.broadcasted_iota(jnp.int32, (tokens, 2 * count), 1)
        named = [ids[:, k : k + 1] == slot for k in range(choose)]
        names = sum(jnp.where(hit, 1.0, 0.0) for hit in named)
        square = (tokens, tokens)
        earlier = lax.broadcasted_iota(jnp.int32, square, 0) > lax.broadcasted_iota(
            jnp.int32, square, 1
        )
        turns = matmul(jnp.where(earlier, 1.0, 0.0).astype(BF), names.astype(BF), 1, 0)
        places = []
        for k in range(choose):
            turn = jnp.sum(jnp.where(named[k], turns, 0.0), axis=1, keepdims=True)
            own = ids[:, k : k + 1]
            kind = jnp.where(own >= count, 1, 0)
            places.append(
                (own - kind * count) * pair + kind * capacity + turn.astype(jnp.int32)
            )
        for n in range(row_tiles):
            shape = (tokens, tile_columns)
            column = lax.broadcasted_iota(jnp.int32, shape, 1) + n * tile_columns
            picks = jnp.zeros(shape, F32)
            weight = jnp.zeros(shape, F32)
            for k in range(choose):
                hit = places[k] == column
                picks = picks + jnp.where(hit, 1.0, 0.0)
                weight = weight + jnp.where(hit, gates[:, k : k + 1], 0.0)
            at = pl.ds(n * tile_columns, tile_columns)
            chosen[:, at] = picks.astype(BF)
            top = weight.astype(BF)
            high[:, at] = top
            low[:, at] = (weight - top.astype(F32)).astype(BF)
            plain = matmul(chosen[:, at], both[...], 0, 0)
            scaled = matmul(high[:, at], both[...], 0, 0) + matmul(low[:, at], both[...], 0, 0)
            lane = lax.broadcasted_iota(jnp.int32, plain.shape, 1)
            sent[pl.ds(n * tile_sources, tile_sources)] = (
                jnp.where(lane < width, plain, scaled)
                .astype(BF)
                .reshape(tile_sources, pair, 2 * width)
            )

    def add_rows():
        plain, scaled = 0.0, 0.0
        for n in range(row_tiles):
            at = pl.ds(n * tile_columns, tile_columns)
            block = returned[pl.ds(n * tile_sources, tile_sources)].reshape(
                tile_columns, 2 * width
            )
            plain = plain + matmul(chosen[:, at], block, 1, 0)
            scaled = scaled + (
                matmul(high[:, at], block, 1, 0) + matmul(low[:, at], block, 1, 0)
            )
        lane = lax.broadcasted_iota(jnp.int32, plain.shape, 1)
        results[...] = jnp.where(lane < width, scaled, plain).astype(BF)

    def sort_rows():
        sources = 8
        for n in range(rows // 128):
            first = min(128 * n // capacity, count - sources)
            block = got[pl.ds(first, sources)].reshape(sources * pair, 2 * width)
            shape = (sources * pair, 128)
            r = lax.broadcasted_iota(jnp.int32, shape, 0)
            lane = lax.broadcasted_iota(jnp.int32, shape, 1) + 128 * n
            inside = lax.rem(r, pair)
            goes_to = (lax.div(r, pair) + first) * capacity + lax.rem(inside, capacity)
            for k in range(2):
                hit = (goes_to == lane) & (lax.div(inside, capacity) == k)
                tile = matmul(block, jnp.where(hit, 1.0, 0.0).astype(BF), 0, 0)
                at = pl.ds(128 * n, 128)
                xs_ref[k, :, at] = tile[:width].astype(BF)
                zs_ref[k, :, at] = tile[width:].astype(BF)

    def unsort_rows(k, first):
        sources, window = 4, 256
        blocks = count // sources

        def block(b):
            start = lax.min(lax.div(b * sources * capacity, 128) * 128, rows - window)
            start = pl.multiple_of(start, 128)
            shape = (sources * pair, window)
            r = lax.broadcasted_iota(jnp.int32, shape, 0)
            lane = lax.broadcasted_iota(jnp.int32, shape, 1) + start
            inside = lax.rem(r, pair)
            comes_from = (lax.div(r, pair) + b * sources) * capacity + lax.rem(inside, capacity)
            hit = (comes_from == lane) & (lax.div(inside, capacity) == k)
            tile = matmul(
                jnp.where(hit, 1.0, 0.0).astype(BF), made[k, :, pl.ds(start, window)], 1, 1
            ).reshape(sources, pair, 2 * width)
            at = pl.ds(b * sources, sources)
            if first:
                got[at] = tile.astype(BF)
            else:
                got[at] = (got[at].astype(F32) + tile).astype(BF)

        each(blocks, 0, block)

    def over_dp(p, acts, early, middle, late):
        def rows_of(c, d=None):
            base = lax.rem(c + 2 * ring, ring) * chunk
            if d is None:
                return pl.ds(pl.multiple_of(base, chunk), chunk)
            return pl.ds(pl.multiple_of(base + d * half, half), half)

        def sum_copy(t, m, d):
            c = z + steps - t if d == 0 else z - steps + t
            if t == 0:
                src = parts.at[p, m, rows_of(c, d)]
                dst = landed.at[p, d, 0, m, pl.ds(d * half, half)]
            else:
                src, dst = landed.at[p, d, t - 1, m], landed.at[p, d, t, m]
            return pltpu.make_async_remote_copy(
                src_ref=src,
                dst_ref=dst,
                send_sem=z_send.at[p, d, t, m],
                recv_sem=z_recv.at[p, d, t, m],
                device_id={"dp": right if d == 0 else left},
                device_id_type=MESH,
            )

        def sum_add(t, m, d):
            c = z + steps - t if d == 0 else z - steps + t
            if t == 1:
                mine, other = pl.ds(d * half, half), pl.ds((1 - d) * half, half)
                landed[p, d, 0, m, mine] = (
                    landed[p, d, 0, m, mine].astype(F32) + parts[p, m, rows_of(c, d)].astype(F32)
                ).astype(BF)
                landed[p, d, 0, m, other] = parts[p, m, rows_of(c, 1 - d)]
            else:
                landed[p, d, t - 1, m] = (
                    landed[p, d, t - 1, m].astype(F32) + parts[p, m, rows_of(c)].astype(F32)
                ).astype(BF)

        def spread_copy(t, m, d):
            c = z - t if d == 0 else z + t
            at = rows_of(c, d) if t == steps - 1 else rows_of(c)
            return pltpu.make_async_remote_copy(
                src_ref=acts.at[m, at],
                dst_ref=acts.at[m, at],
                send_sem=g_send.at[p, d, t, m],
                recv_sem=g_recv.at[p, d, t, m],
                device_id={"dp": right if d == 0 else left},
                device_id_type=MESH,
            )

        in_flight = ([], [])

        def launch(copy, d):
            if len(in_flight[d]) == DEPTH:
                in_flight[d].pop(0).wait_send()
            copy.start()
            in_flight[d].append(copy)

        for m in range(3):
            for d in sides:
                launch(sum_copy(0, m, d), d)
        early()
        for t in range(1, steps):
            for m in range(3):
                for d in sides:
                    sum_copy(t - 1, m, d).wait_recv()
                    sum_add(t, m, d)
                    launch(sum_copy(t, m, d), d)

        def total(m):
            for d in sides:
                sum_copy(steps - 1, m, d).wait_recv()
            return (
                landed[p, 0, steps - 1, m].astype(F32)
                + landed[p, 1, steps - 1, m].astype(F32)
                + parts[p, m, rows_of(z)].astype(F32)
            )

        def spread_first(m, value):
            acts[m, rows_of(z)] = value.astype(BF)
            for d in sides:
                launch(spread_copy(0, m, d), d)

        gate = total(0)
        up = total(1)
        q = jax.nn.sigmoid(gate)
        silu = gate * q
        spread_first(2, silu * up)
        grad = total(2)
        spread_first(0, grad * up * q * (1.0 + gate * (1.0 - q)))
        spread_first(1, grad * silu)
        middle()
        for t in range(1, steps):
            for m in (2, 0, 1):
                for d in sides:
                    spread_copy(t - 1, m, d).wait_recv()
                    launch(spread_copy(t, m, d), d)
            if t == 1:
                late()
        for m in (2, 0, 1):
            for d in sides:
                spread_copy(steps - 1, m, d).wait_recv()
        for d in sides:
            for copy in in_flight[d]:
                copy.wait_send()

    def nothing():
        pass

    moves = [
        Move(0, weights.at[0], copied.at[0], False),
        Move(1, weights.at[1], copied.at[1], False),
        Move(2, slot_grads.at[0], summed.at[0], True),
        Move(3, slot_grads.at[1], summed.at[1], True),
    ]
    for m in range(3):
        place_copy(0, m).wait()
    moves[0].begin()
    send_rows()
    exchange(sent, got, 0)()
    moves[0].pass_on()
    sort_rows()
    multiply_parts(weights.at[0], 0, 0)
    for m in range(3):
        place_copy(1, m).wait()

    def next_weights():
        moves[0].finish()
        moves[1].begin()

    over_dp(0, home_acts.at[0], nothing, next_weights, nothing)
    multiply_parts(copied.at[0], 1, 1)

    def home_rows():
        moves[1].pass_on()
        multiply_rows(weights.at[0], home_acts.at[0], keep_rows(0))

    over_dp(1, rep_acts.at[0], home_rows, nothing, nothing)
    moves[1].finish()
    multiply_parts(copied.at[1], 1, 0)

    def first_grads():
        multiply_grads(rep_acts.at[0], 1, slot_grads.at[0])
        moves[2].begin()
        multiply_rows(copied.at[0], rep_acts.at[0], keep_rows(1))

    over_dp(0, rep_acts.at[1], first_grads, moves[2].pass_on, nothing)
    multiply_parts(weights.at[1], 0, 1)
    moves[2].finish()

    def second_grads():
        multiply_grads(rep_acts.at[1], 1, slot_grads.at[1])
        moves[3].begin()

    def replica_rows():
        multiply_rows(copied.at[1], rep_acts.at[1], end_rows(1))
        unsort_rows(1, True)

    over_dp(1, home_acts.at[1], second_grads, moves[3].pass_on, replica_rows)
    multiply_rows(weights.at[1], home_acts.at[1], end_rows(0))
    unsort_rows(0, False)
    done = exchange(got, returned, 1)
    home_grads(0)
    moves[3].finish()
    home_grads(1)
    done()
    add_rows()


def layer(plan, before_it, last_of, ids, gates, both, w_gate, w_up, w_down, capacity, ring):
    count = plan.shape[0]
    tokens, two_width = both.shape
    width, hidden = w_gate.shape
    half_hidden = hidden // 2
    pair = 2 * capacity
    rows = count * capacity
    columns = count * pair
    flat = -(-3 * width // (8 * 16)) * 8 * 16
    steps = ring // 2
    chunk = half_hidden // ring
    piece = (flat // 8, half_hidden * 8 // count)
    sem = pltpu.SemaphoreType.DMA
    acts = (2, 3, half_hidden, rows)
    halves = (2, flat, half_hidden)
    blocks = (count, pair, two_width)
    return pl.pallas_call(
        functools.partial(layer_kernel, count, ring, capacity),
        out_shape=(
            jax.ShapeDtypeStruct((tokens, two_width), BF),
            jax.ShapeDtypeStruct((3 * width, hidden), F32),
        ),
        in_specs=[pl.BlockSpec(memory_space=pltpu.SMEM)] * 3
        + [pl.BlockSpec(memory_space=VMEM)] * 3
        + [pl.BlockSpec(memory_space=pl.ANY)] * 3,
        out_specs=[pl.BlockSpec(memory_space=VMEM)] * 2,
        scratch_shapes=[
            VMEM(halves, BF),
            VMEM(blocks, BF),
            VMEM(blocks, BF),
            VMEM((tokens, columns), BF),
            VMEM((tokens, columns), BF),
            VMEM((tokens, columns), BF),
            VMEM(blocks, BF),
            VMEM(acts, BF),
            VMEM(halves, BF),
            VMEM((2, width, rows), BF),
            VMEM((2, width, rows), BF),
            VMEM(halves, BF),
            VMEM((2, 3, half_hidden, rows), BF),
            VMEM(acts, BF),
            VMEM((2, 2, steps, 3, chunk, rows), BF),
            VMEM((count,) + piece, BF),
            VMEM((count,) + piece, BF),
            VMEM((2, count) + piece, BF),
            VMEM((count,) + piece, F32),
            VMEM(halves, BF),
            VMEM((2, two_width, rows), F32),
            VMEM((2, two_width, rows), BF),
            sem((2, 2, steps, 3)),
            sem((2, 2, steps, 3)),
            sem((2, 2, steps, 3)),
            sem((2, 2, steps, 3)),
            sem((2, count)),
            sem((2, count)),
            sem((2, count)),
            sem((2, count)),
            sem((2, count)),
            sem((2, count)),
            sem((4,)),
            sem((2, 3)),
        ],
        compiler_params=pltpu.CompilerParams(
            collective_id=1, has_side_effects=True, vmem_limit_bytes=63 << 20
        ),
        name="layer",
    )(plan, before_it, last_of, ids, gates, both, w_gate, w_up, w_down)


def body(tokens, cotangent, slot_ids, gates, plan, w_gate, w_up, w_down):
    count = lax.axis_size("expert")
    ring = lax.axis_size("dp")
    token_count, width = tokens.shape
    capacity = 5 * token_count * slot_ids.shape[1] // (4 * 2 * count)

    s_ids = jnp.arange(count, dtype=jnp.int32)
    alike = (plan[None, :] == plan[:, None]) & (s_ids[None, :] < s_ids[:, None])
    before_it = jnp.max(jnp.where(alike, s_ids[None, :], -1), axis=1)
    last_of = jnp.max(jnp.where(plan[None, :] == s_ids[:, None], s_ids[None, :], -1), axis=1)

    results, grads = layer(
        plan,
        before_it,
        last_of,
        slot_ids,
        gates,
        jnp.concatenate([tokens, cotangent], axis=1),
        w_gate[0],
        w_up[0],
        jnp.swapaxes(w_down[0], 0, 1),
        capacity,
        ring,
    )
    return (
        results[:, :width],
        results[:, width:],
        grads[:width][None],
        grads[width : 2 * width][None],
        jnp.swapaxes(grads[2 * width :], 0, 1)[None],
    )


def solution(mesh):
    in_specs = (
        P("expert", "dp"),
        P("expert", "dp"),
        P("expert", None),
        P("expert", None),
        P(),
        P("expert", "dp", None),
        P("expert", "dp", None),
        P("expert", None, "dp"),
    )
    out_specs = (
        P("expert", "dp"),
        P("expert", "dp"),
        P("expert", "dp", None),
        P("expert", "dp", None),
        P("expert", None, "dp"),
    )
    return jax.shard_map(body, mesh=mesh, in_specs=in_specs, out_specs=out_specs, check_vma=False)
```

```python
import functools

import jax
import jax.numpy as jnp
from jax import lax
from jax.experimental import pallas as pl
from jax.experimental.pallas import tpu as pltpu
from jax.sharding import PartitionSpec as P

MESH = pl.DeviceIdType.MESH
BF = jnp.bfloat16
F32 = jnp.float32
VMEM = pltpu.VMEM
DEPTH = 2
STRIDE = 11


def greet(axis, peers):
    barrier = pltpu.get_barrier_semaphore()
    for peer in peers:
        pl.semaphore_signal(barrier, inc=1, device_id={axis: peer}, device_id_type=MESH)


def greet_all(axis, count, me):
    barrier = pltpu.get_barrier_semaphore()

    def one(i, carry):
        pl.semaphore_signal(
            barrier, inc=1, device_id={axis: lax.rem(me + i, count)}, device_id_type=MESH
        )
        return carry

    lax.fori_loop(1, count, one, 0)


def each(count, first, function):
    def step(i, carry):
        function(i)
        return carry

    lax.fori_loop(first, count, step, 0)


def matmul(a, b, ca, cb):
    return lax.dot_general(a, b, (((ca,), (cb,)), ((), ())), preferred_element_type=F32)


def layer_kernel(
    count, ring, capacity, plan, before_it, last_of, ids, gates, both, w_gate, w_up, w_down,
    results, grads,
    weights, sent, returned, chosen, high, low, got, home_acts, summed, xs_ref, zs_ref, copied, parts, rep_acts, landed, held_even, held_odd, staged, run, slot_grads, rows_acc, made,
    z_send, z_recv, g_send, g_recv, out_send, out_recv, back_send, back_recv, ex_send, ex_recv, local, placed,
):
    me = lax.axis_index("expert")
    z = lax.axis_index("dp")
    right, left = lax.rem(z + 1, ring), lax.rem(z + ring - 1, ring)
    width, rows = xs_ref.shape[1], xs_ref.shape[2]
    half_hidden = parts.shape[2]
    chunk = half_hidden // ring
    half = chunk // 2
    steps = ring // 2
    pair = 2 * capacity
    row_blocks = 8
    lane_blocks = count // row_blocks
    piece_rows, piece = held_even.shape[1], held_even.shape[2]
    sides = (0, 1)

    def place_copy(h, m):
        lane = pl.ds(h * half_hidden, half_hidden)
        return pltpu.make_async_copy(
            (w_gate, w_up, w_down)[m].at[:, lane],
            weights.at[h, pl.ds(m * width, width)],
            placed.at[h, m],
        )

    for h in range(2):
        for m in range(3):
            place_copy(h, m).start()
    greet("dp", (right, left))
    greet_all("expert", count, me)
    pad = weights.shape[1] - 3 * width
    if pad:
        for h in range(2):
            for ref in (weights, slot_grads):
                ref[h, pl.ds(3 * width, pad)] = jnp.zeros((pad, half_hidden), BF)
    pl.semaphore_wait(pltpu.get_barrier_semaphore(), count + 1)

    def peer_of(i):
        return lax.rem(me + STRIDE * i, count)

    def to_peer(src, dst, send, recv, peer):
        return pltpu.make_async_remote_copy(
            src_ref=src, dst_ref=dst, send_sem=send, recv_sem=recv,
            device_id={"expert": peer}, device_id_type=MESH,
        )

    split = -(-width // 128) * 128

    def exchange(src, dst, turn, first=0, stop=2 * width):
        lanes = pl.ds(first, stop - first)

        def copy(i):
            peer = peer_of(i)
            return to_peer(
                src.at[peer, :, lanes],
                dst.at[me, :, lanes],
                ex_send.at[turn, i],
                ex_recv.at[turn, i],
                peer,
            )

        own = pltpu.make_async_copy(
            src.at[me, :, lanes], dst.at[me, :, lanes], local.at[2 + turn]
        )
        own.start()
        each(count, 1, lambda i: copy(i).start())

        def finish():
            own.wait()
            each(count, 1, lambda i: copy(i).wait())

        return finish

    def part_of(block):
        row = pl.multiple_of(lax.div(block, lane_blocks) * piece_rows, 16)
        lane = pl.multiple_of(lax.rem(block, lane_blocks) * piece, piece)
        return (pl.ds(row, piece_rows), pl.ds(lane, piece))

    class Move:
        def __init__(self, turn, source, result, summing):
            self.p, self.source, self.result, self.summing = turn % 2, source, result, summing
            self.held = held_odd if self.p else held_even

        def out_copy(self, i):
            peer = peer_of(i)
            return to_peer(
                self.source.at[part_of(peer)], self.held.at[me],
                out_send.at[self.p, i], out_recv.at[self.p, i], peer,
            )

        def back_copy(self, i):
            peer = peer_of(i)
            return to_peer(
                staged.at[self.p, peer], self.result.at[part_of(me)],
                back_send.at[self.p, i], back_recv.at[self.p, i], peer,
            )

        def own_out(self):
            return pltpu.make_async_copy(
                self.source.at[part_of(me)], self.held.at[me], local.at[0]
            )

        def own_back(self):
            return pltpu.make_async_copy(
                staged.at[self.p, me], self.result.at[part_of(me)], local.at[1]
            )

        def begin(self, first=1, stop=count):
            if first == 1:
                self.own_out().start()
            each(stop, first, lambda i: self.out_copy(i).start())

        def pass_on(self):
            self.own_out().wait()
            each(count, 1, lambda i: self.out_copy(i).wait())
            if self.summing:
                run[0] = self.held[0].astype(F32)

                def add(r):
                    prior = before_it[r]
                    keep = jnp.where(prior >= 0, 1.0, 0.0)
                    run[r] = run[jnp.maximum(prior, 0)] * keep + self.held[r].astype(F32)

                each(count, 1, add)

            def fill(i):
                s = peer_of(i)
                if self.summing:
                    final = last_of[s]
                    some = jnp.where(final >= 0, 1.0, 0.0)
                    staged[self.p, s] = (run[jnp.maximum(final, 0)] * some).astype(BF)
                else:
                    staged[self.p, s] = self.held[plan[s]]

            fill(0)
            self.own_back().start()

            def fill_and_send(i):
                fill(i)
                self.back_copy(i).start()

            each(count, 1, fill_and_send)

        def finish(self):
            self.own_back().wait()
            each(count, 1, lambda i: self.back_copy(i).wait())

    lane_tile = half_hidden // 2

    def multiply_part(w, k, p, m):
        src = zs_ref if m == 2 else xs_ref

        def tile(b):
            lane = pl.ds(pl.multiple_of(b * lane_tile, lane_tile), lane_tile)
            parts[p, m, lane] = matmul(w[pl.ds(m * width, width), lane], src[k], 0, 0).astype(BF)

        each(2, 0, tile)

    tile_rows = width // 2

    def multiply_grads(acts, k, dst):
        for m in range(3):
            src = zs_ref if m == 2 else xs_ref

            def tile(b, m=m, src=src):
                row = pl.multiple_of(b * tile_rows, tile_rows)
                dst[pl.ds(m * width + row, tile_rows)] = matmul(
                    src[k, pl.ds(row, tile_rows)], acts[m], 1, 1
                ).astype(BF)

            each(2, 0, tile)

    def home_grads(h):
        lane = pl.ds(h * half_hidden, half_hidden)
        for m in range(3):
            src = zs_ref if m == 2 else xs_ref

            def tile(b, m=m, src=src):
                row = pl.multiple_of(b * tile_rows, tile_rows)
                at = pl.ds(m * width + row, tile_rows)
                grads[at, lane] = matmul(
                    src[0, pl.ds(row, tile_rows)], home_acts[h, m], 1, 1
                ) + summed[h, at].astype(F32)

            each(2, 0, tile)

    def multiply_rows(w, acts, store):
        def tile(b):
            row = pl.multiple_of(b * tile_rows, tile_rows)
            down = pl.ds(2 * width + row, tile_rows)
            store(row, matmul(w[down], acts[2], 1, 0))
            up = pl.ds(width + row, tile_rows)
            store(
                width + row,
                matmul(w[pl.ds(row, tile_rows)], acts[0], 1, 0)
                + matmul(w[up], acts[1], 1, 0),
            )

        each(2, 0, tile)

    def keep_rows(k):
        def store(row, value):
            rows_acc[k, pl.ds(row, tile_rows)] = value

        return store

    def end_rows(k):
        def store(row, value):
            at = pl.ds(row, tile_rows)
            made[k, at] = (rows_acc[k, at] + value).astype(BF)

        return store

    row_tiles = 2
    tile_columns = count * pair // row_tiles
    tile_sources = count // row_tiles

    def send_rows():
        tokens, choose = ids.shape
        slot = lax.broadcasted_iota(jnp.int32, (tokens, 2 * count), 1)
        named = [ids[:, k : k + 1] == slot for k in range(choose)]
        names = sum(jnp.where(hit, 1.0, 0.0) for hit in named)
        square = (tokens, tokens)
        earlier = lax.broadcasted_iota(jnp.int32, square, 0) > lax.broadcasted_iota(
            jnp.int32, square, 1
        )
        turns = matmul(jnp.where(earlier, 1.0, 0.0).astype(BF), names.astype(BF), 1, 0)
        places = []
        for k in range(choose):
            turn = jnp.sum(jnp.where(named[k], turns, 0.0), axis=1, keepdims=True)
            own = ids[:, k : k + 1]
            kind = jnp.where(own >= count, 1, 0)
            places.append(
                (own - kind * count) * pair + kind * capacity + turn.astype(jnp.int32)
            )
        for n in range(row_tiles):
            shape = (tokens, tile_columns)
            column = lax.broadcasted_iota(jnp.int32, shape, 1) + n * tile_columns
            picks = jnp.zeros(shape, F32)
            weight = jnp.zeros(shape, F32)
            for k in range(choose):
                hit = places[k] == column
                picks = picks + jnp.where(hit, 1.0, 0.0)
                weight = weight + jnp.where(hit, gates[:, k : k + 1], 0.0)
            at = pl.ds(n * tile_columns, tile_columns)
            chosen[:, at] = picks.astype(BF)
            top = weight.astype(BF)
            high[:, at] = top
            low[:, at] = (weight - top.astype(F32)).astype(BF)
            plain = matmul(chosen[:, at], both[...], 0, 0)
            scaled = matmul(high[:, at], both[...], 0, 0) + matmul(low[:, at], both[...], 0, 0)
            lane = lax.broadcasted_iota(jnp.int32, plain.shape, 1)
            sent[pl.ds(n * tile_sources, tile_sources)] = (
                jnp.where(lane < width, plain, scaled)
                .astype(BF)
                .reshape(tile_sources, pair, 2 * width)
            )

    def add_rows():
        plain, scaled = 0.0, 0.0
        for n in range(row_tiles):
            at = pl.ds(n * tile_columns, tile_columns)
            block = returned[pl.ds(n * tile_sources, tile_sources)].reshape(
                tile_columns, 2 * width
            )
            plain = plain + matmul(chosen[:, at], block, 1, 0)
            scaled = scaled + (
                matmul(high[:, at], block, 1, 0) + matmul(low[:, at], block, 1, 0)
            )
        lane = lax.broadcasted_iota(jnp.int32, plain.shape, 1)
        results[...] = jnp.where(lane < width, scaled, plain).astype(BF)

    def sort_rows(ref, first_lane, skip):
        sources = 8
        for n in range(rows // 128):
            first = min(128 * n // capacity, count - sources)
            block = got[pl.ds(first, sources), :, pl.ds(first_lane, split)].reshape(
                sources * pair, split
            )
            shape = (sources * pair, 128)
            r = lax.broadcasted_iota(jnp.int32, shape, 0)
            lane = lax.broadcasted_iota(jnp.int32, shape, 1) + 128 * n
            inside = lax.rem(r, pair)
            goes_to = (lax.div(r, pair) + first) * capacity + lax.rem(inside, capacity)
            for k in range(2):
                hit = (goes_to == lane) & (lax.div(inside, capacity) == k)
                tile = matmul(block, jnp.where(hit, 1.0, 0.0).astype(BF), 0, 0)
                ref[k, :, pl.ds(128 * n, 128)] = tile[skip : skip + width].astype(BF)

    def unsort_rows(k, first):
        sources, window = 4, 256
        blocks = count // sources

        def block(b):
            start = lax.min(lax.div(b * sources * capacity, 128) * 128, rows - window)
            start = pl.multiple_of(start, 128)
            shape = (sources * pair, window)
            r = lax.broadcasted_iota(jnp.int32, shape, 0)
            lane = lax.broadcasted_iota(jnp.int32, shape, 1) + start
            inside = lax.rem(r, pair)
            comes_from = (lax.div(r, pair) + b * sources) * capacity + lax.rem(inside, capacity)
            hit = (comes_from == lane) & (lax.div(inside, capacity) == k)
            tile = matmul(
                jnp.where(hit, 1.0, 0.0).astype(BF), made[k, :, pl.ds(start, window)], 1, 1
            ).reshape(sources, pair, 2 * width)
            at = pl.ds(b * sources, sources)
            if first:
                got[at] = tile.astype(BF)
            else:
                got[at] = (got[at].astype(F32) + tile).astype(BF)

        each(blocks, 0, block)

    def over_dp(p, acts, prepare, early, middle, late):
        def rows_of(c, d=None):
            base = lax.rem(c + 2 * ring, ring) * chunk
            if d is None:
                return pl.ds(pl.multiple_of(base, chunk), chunk)
            return pl.ds(pl.multiple_of(base + d * half, half), half)

        def sum_copy(t, m, d):
            c = z + steps - t if d == 0 else z - steps + t
            if t == 0:
                src = parts.at[p, m, rows_of(c, d)]
                dst = landed.at[p, d, 0, m, pl.ds(d * half, half)]
            else:
                src, dst = landed.at[p, d, t - 1, m], landed.at[p, d, t, m]
            return pltpu.make_async_remote_copy(
                src_ref=src,
                dst_ref=dst,
                send_sem=z_send.at[p, d, t, m],
                recv_sem=z_recv.at[p, d, t, m],
                device_id={"dp": right if d == 0 else left},
                device_id_type=MESH,
            )

        def sum_add(t, m, d):
            c = z + steps - t if d == 0 else z - steps + t
            if t == 1:
                mine, other = pl.ds(d * half, half), pl.ds((1 - d) * half, half)
                landed[p, d, 0, m, mine] = (
                    landed[p, d, 0, m, mine].astype(F32) + parts[p, m, rows_of(c, d)].astype(F32)
                ).astype(BF)
                landed[p, d, 0, m, other] = parts[p, m, rows_of(c, 1 - d)]
            else:
                landed[p, d, t - 1, m] = (
                    landed[p, d, t - 1, m].astype(F32) + parts[p, m, rows_of(c)].astype(F32)
                ).astype(BF)

        def spread_copy(t, m, d):
            c = z - t if d == 0 else z + t
            at = rows_of(c, d) if t == steps - 1 else rows_of(c)
            return pltpu.make_async_remote_copy(
                src_ref=acts.at[m, at],
                dst_ref=acts.at[m, at],
                send_sem=g_send.at[p, d, t, m],
                recv_sem=g_recv.at[p, d, t, m],
                device_id={"dp": right if d == 0 else left},
                device_id_type=MESH,
            )

        in_flight = ([], [])

        def launch(copy, d):
            if len(in_flight[d]) == DEPTH:
                in_flight[d].pop(0).wait_send()
            copy.start()
            in_flight[d].append(copy)

        for m in range(3):
            prepare(m)
            for d in sides:
                launch(sum_copy(0, m, d), d)
        early()
        for t in range(1, steps):
            for m in range(3):
                for d in sides:
                    sum_copy(t - 1, m, d).wait_recv()
                    sum_add(t, m, d)
                    launch(sum_copy(t, m, d), d)

        def total(m):
            for d in sides:
                sum_copy(steps - 1, m, d).wait_recv()
            return (
                landed[p, 0, steps - 1, m].astype(F32)
                + landed[p, 1, steps - 1, m].astype(F32)
                + parts[p, m, rows_of(z)].astype(F32)
            )

        def spread_first(m, value):
            acts[m, rows_of(z)] = value.astype(BF)
            for d in sides:
                launch(spread_copy(0, m, d), d)

        gate = total(0)
        up = total(1)
        q = jax.nn.sigmoid(gate)
        silu = gate * q
        spread_first(2, silu * up)
        grad = total(2)
        spread_first(0, grad * up * q * (1.0 + gate * (1.0 - q)))
        spread_first(1, grad * silu)
        middle()
        for t in range(1, steps):
            for m in (2, 0, 1):
                for d in sides:
                    spread_copy(t - 1, m, d).wait_recv()
                    launch(spread_copy(t, m, d), d)
            if t in late:
                late[t]()
        for m in (2, 0, 1):
            for d in sides:
                spread_copy(steps - 1, m, d).wait_recv()
        for d in sides:
            for copy in in_flight[d]:
                copy.wait_send()

    def nothing():
        pass

    moves = [
        Move(0, weights.at[0], copied.at[0], False),
        Move(1, weights.at[1], copied.at[1], False),
        Move(2, slot_grads.at[0], summed.at[0], True),
        Move(3, slot_grads.at[1], summed.at[1], True),
    ]
    for m in range(3):
        place_copy(0, m).wait()
    moves[0].begin(1, count // 2)
    send_rows()
    exchange(sent, got, 0, 0, split)()
    others = exchange(sent, got, 1, split)

    def first_inputs(m):
        if m == 0:
            sort_rows(xs_ref, 0, 0)
        if m == 2:
            others()
            sort_rows(zs_ref, 2 * width - split, split - width)
        multiply_part(weights.at[0], 0, 0, m)

    def more_weights():
        moves[0].begin(count // 2, count)
        for m in range(3):
            place_copy(1, m).wait()

    over_dp(0, home_acts.at[0], first_inputs, more_weights, moves[0].pass_on, {})
    moves[0].finish()
    moves[1].begin()
    over_dp(
        1,
        rep_acts.at[0],
        lambda m: multiply_part(copied.at[0], 1, 1, m),
        nothing,
        moves[1].pass_on,
        {1: lambda: multiply_rows(weights.at[0], home_acts.at[0], keep_rows(0))},
    )
    moves[1].finish()

    def first_grads():
        multiply_grads(rep_acts.at[0], 1, slot_grads.at[0])
        moves[2].begin()

    over_dp(
        0,
        rep_acts.at[1],
        lambda m: multiply_part(copied.at[1], 1, 0, m),
        first_grads,
        moves[2].pass_on,
        {1: lambda: multiply_rows(copied.at[0], rep_acts.at[0], keep_rows(1))},
    )

    def second_grads():
        moves[2].finish()
        multiply_grads(rep_acts.at[1], 1, slot_grads.at[1])
        moves[3].begin()

    over_dp(
        1,
        home_acts.at[1],
        lambda m: multiply_part(weights.at[1], 0, 1, m),
        second_grads,
        moves[3].pass_on,
        {
            1: lambda: multiply_rows(copied.at[1], rep_acts.at[1], end_rows(1)),
            2: lambda: unsort_rows(1, True),
        },
    )
    multiply_rows(weights.at[1], home_acts.at[1], end_rows(0))
    unsort_rows(0, False)
    done = exchange(got, returned, 2)
    home_grads(0)
    moves[3].finish()
    home_grads(1)
    done()
    add_rows()


def layer(plan, before_it, last_of, ids, gates, both, w_gate, w_up, w_down, capacity, ring):
    count = plan.shape[0]
    tokens, two_width = both.shape
    width, hidden = w_gate.shape
    half_hidden = hidden // 2
    pair = 2 * capacity
    rows = count * capacity
    columns = count * pair
    flat = -(-3 * width // (8 * 16)) * 8 * 16
    steps = ring // 2
    chunk = half_hidden // ring
    piece = (flat // 8, half_hidden * 8 // count)
    sem = pltpu.SemaphoreType.DMA
    acts = (2, 3, half_hidden, rows)
    halves = (2, flat, half_hidden)
    blocks = (count, pair, two_width)
    return pl.pallas_call(
        functools.partial(layer_kernel, count, ring, capacity),
        out_shape=(
            jax.ShapeDtypeStruct((tokens, two_width), BF),
            jax.ShapeDtypeStruct((3 * width, hidden), F32),
        ),
        in_specs=[pl.BlockSpec(memory_space=pltpu.SMEM)] * 3
        + [pl.BlockSpec(memory_space=VMEM)] * 3
        + [pl.BlockSpec(memory_space=pl.ANY)] * 3,
        out_specs=[pl.BlockSpec(memory_space=VMEM)] * 2,
        scratch_shapes=[
            VMEM(halves, BF),
            VMEM(blocks, BF),
            VMEM(blocks, BF),
            VMEM((tokens, columns), BF),
            VMEM((tokens, columns), BF),
            VMEM((tokens, columns), BF),
            VMEM(blocks, BF),
            VMEM(acts, BF),
            VMEM(halves, BF),
            VMEM((2, width, rows), BF),
            VMEM((2, width, rows), BF),
            VMEM(halves, BF),
            VMEM((2, 3, half_hidden, rows), BF),
            VMEM(acts, BF),
            VMEM((2, 2, steps, 3, chunk, rows), BF),
            VMEM((count,) + piece, BF),
            VMEM((count,) + piece, BF),
            VMEM((2, count) + piece, BF),
            VMEM((count,) + piece, F32),
            VMEM(halves, BF),
            VMEM((2, two_width, rows), F32),
            VMEM((2, two_width, rows), BF),
            sem((2, 2, steps, 3)),
            sem((2, 2, steps, 3)),
            sem((2, 2, steps, 3)),
            sem((2, 2, steps, 3)),
            sem((2, count)),
            sem((2, count)),
            sem((2, count)),
            sem((2, count)),
            sem((3, count)),
            sem((3, count)),
            sem((5,)),
            sem((2, 3)),
        ],
        compiler_params=pltpu.CompilerParams(
            collective_id=1, has_side_effects=True, vmem_limit_bytes=63 << 20
        ),
        name="layer",
    )(plan, before_it, last_of, ids, gates, both, w_gate, w_up, w_down)


def body(tokens, cotangent, slot_ids, gates, plan, w_gate, w_up, w_down):
    count = lax.axis_size("expert")
    ring = lax.axis_size("dp")
    token_count, width = tokens.shape
    capacity = 5 * token_count * slot_ids.shape[1] // (4 * 2 * count)

    s_ids = jnp.arange(count, dtype=jnp.int32)
    alike = (plan[None, :] == plan[:, None]) & (s_ids[None, :] < s_ids[:, None])
    before_it = jnp.max(jnp.where(alike, s_ids[None, :], -1), axis=1)
    last_of = jnp.max(jnp.where(plan[None, :] == s_ids[:, None], s_ids[None, :], -1), axis=1)

    results, grads = layer(
        plan,
        before_it,
        last_of,
        slot_ids,
        gates,
        jnp.concatenate([tokens, cotangent], axis=1),
        w_gate[0],
        w_up[0],
        jnp.swapaxes(w_down[0], 0, 1),
        capacity,
        ring,
    )
    return (
        results[:, :width],
        results[:, width:],
        grads[:width][None],
        grads[width : 2 * width][None],
        jnp.swapaxes(grads[2 * width :], 0, 1)[None],
    )


def solution(mesh):
    in_specs = (
        P("expert", "dp"),
        P("expert", "dp"),
        P("expert", None),
        P("expert", None),
        P(),
        P("expert", "dp", None),
        P("expert", "dp", None),
        P("expert", None, "dp"),
    )
    out_specs = (
        P("expert", "dp"),
        P("expert", "dp"),
        P("expert", "dp", None),
        P("expert", "dp", None),
        P("expert", None, "dp"),
    )
    return jax.shard_map(body, mesh=mesh, in_specs=in_specs, out_specs=out_specs, check_vma=False)
```

```python
import functools

import jax
import jax.numpy as jnp
from jax import lax
from jax.experimental import pallas as pl
from jax.experimental.pallas import tpu as pltpu
from jax.sharding import PartitionSpec as P

MESH = pl.DeviceIdType.MESH
BF = jnp.bfloat16
F32 = jnp.float32
VMEM = pltpu.VMEM
DEPTH = 2
STRIDE = 11


def greet(axis, peers):
    barrier = pltpu.get_barrier_semaphore()
    for peer in peers:
        pl.semaphore_signal(barrier, inc=1, device_id={axis: peer}, device_id_type=MESH)


def greet_all(axis, count, me):
    barrier = pltpu.get_barrier_semaphore()

    def one(i, carry):
        pl.semaphore_signal(
            barrier, inc=1, device_id={axis: lax.rem(me + i, count)}, device_id_type=MESH
        )
        return carry

    lax.fori_loop(1, count, one, 0)


def each(count, first, function):
    def step(i, carry):
        function(i)
        return carry

    lax.fori_loop(first, count, step, 0)


def matmul(a, b, ca, cb):
    return lax.dot_general(a, b, (((ca,), (cb,)), ((), ())), preferred_element_type=F32)


def layer_kernel(
    count, ring, capacity, plan, before_it, last_of, ids_t, gates_t, tokens_t, cotangent_t, w_gate, w_up, w_down,
    output_t, token_grad_t, grads,
    weights, sent, returned, chosen, high, low, got, home_acts, summed, xs_ref, zs_ref, copied, parts, rep_acts, landed, held_even, held_odd, staged, run, slot_grads, rows_acc, made,
    z_send, z_recv, g_send, g_recv, out_send, out_recv, back_send, back_recv, ex_send, ex_recv, local, placed,
):
    me = lax.axis_index("expert")
    z = lax.axis_index("dp")
    right, left = lax.rem(z + 1, ring), lax.rem(z + ring - 1, ring)
    width, rows = xs_ref.shape[1], xs_ref.shape[2]
    half_hidden = parts.shape[2]
    chunk = half_hidden // ring
    half = chunk // 2
    steps = ring // 2
    pair = 2 * capacity
    row_blocks = 8
    lane_blocks = count // row_blocks
    piece_rows, piece = held_even.shape[1], held_even.shape[2]
    sides = (0, 1)

    def place_copy(h, m):
        lane = pl.ds(h * half_hidden, half_hidden)
        return pltpu.make_async_copy(
            (w_gate, w_up, w_down)[m].at[:, lane],
            weights.at[h, pl.ds(m * width, width)],
            placed.at[h, m],
        )

    for h in range(2):
        for m in range(3):
            place_copy(h, m).start()
    greet("dp", (right, left))
    greet_all("expert", count, me)
    pad = weights.shape[1] - 3 * width
    if pad:
        for h in range(2):
            for ref in (weights, slot_grads):
                ref[h, pl.ds(3 * width, pad)] = jnp.zeros((pad, half_hidden), BF)
    pl.semaphore_wait(pltpu.get_barrier_semaphore(), count + 1)

    def peer_of(i):
        return lax.rem(me + STRIDE * i, count)

    def to_peer(src, dst, send, recv, peer):
        return pltpu.make_async_remote_copy(
            src_ref=src, dst_ref=dst, send_sem=send, recv_sem=recv,
            device_id={"expert": peer}, device_id_type=MESH,
        )

    split = -(-width // 128) * 128

    def exchange(src, dst, turn, first=0, stop=2 * width):
        lanes = pl.ds(first, stop - first)

        def copy(i):
            peer = peer_of(i)
            return to_peer(
                src.at[peer, :, lanes],
                dst.at[me, :, lanes],
                ex_send.at[turn, i],
                ex_recv.at[turn, i],
                peer,
            )

        own = pltpu.make_async_copy(
            src.at[me, :, lanes], dst.at[me, :, lanes], local.at[2 + turn]
        )
        own.start()
        each(count, 1, lambda i: copy(i).start())

        def finish():
            own.wait()
            each(count, 1, lambda i: copy(i).wait())

        return finish

    def part_of(block):
        row = pl.multiple_of(lax.div(block, lane_blocks) * piece_rows, 16)
        lane = pl.multiple_of(lax.rem(block, lane_blocks) * piece, piece)
        return (pl.ds(row, piece_rows), pl.ds(lane, piece))

    class Move:
        def __init__(self, turn, source, result, summing):
            self.p, self.source, self.result, self.summing = turn % 2, source, result, summing
            self.held = held_odd if self.p else held_even

        def out_copy(self, i):
            peer = peer_of(i)
            return to_peer(
                self.source.at[part_of(peer)], self.held.at[me],
                out_send.at[self.p, i], out_recv.at[self.p, i], peer,
            )

        def back_copy(self, i):
            peer = peer_of(i)
            return to_peer(
                staged.at[self.p, peer], self.result.at[part_of(me)],
                back_send.at[self.p, i], back_recv.at[self.p, i], peer,
            )

        def own_out(self):
            return pltpu.make_async_copy(
                self.source.at[part_of(me)], self.held.at[me], local.at[0]
            )

        def own_back(self):
            return pltpu.make_async_copy(
                staged.at[self.p, me], self.result.at[part_of(me)], local.at[1]
            )

        def begin(self, first=1, stop=count):
            if first == 1:
                self.own_out().start()
            each(stop, first, lambda i: self.out_copy(i).start())

        def pass_on(self):
            self.own_out().wait()
            each(count, 1, lambda i: self.out_copy(i).wait())
            if self.summing:
                run[0] = self.held[0].astype(F32)

                def add(r):
                    prior = before_it[r]
                    keep = jnp.where(prior >= 0, 1.0, 0.0)
                    run[r] = run[jnp.maximum(prior, 0)] * keep + self.held[r].astype(F32)

                each(count, 1, add)

            def fill(i):
                s = peer_of(i)
                if self.summing:
                    final = last_of[s]
                    some = jnp.where(final >= 0, 1.0, 0.0)
                    staged[self.p, s] = (run[jnp.maximum(final, 0)] * some).astype(BF)
                else:
                    staged[self.p, s] = self.held[plan[s]]

            fill(0)
            self.own_back().start()

            def fill_and_send(i):
                fill(i)
                self.back_copy(i).start()

            each(count, 1, fill_and_send)

        def finish(self):
            self.own_back().wait()
            each(count, 1, lambda i: self.back_copy(i).wait())

    lane_tile = half_hidden // 2

    def multiply_part(w, k, p, m):
        src = zs_ref if m == 2 else xs_ref

        def tile(b):
            lane = pl.ds(pl.multiple_of(b * lane_tile, lane_tile), lane_tile)
            parts[p, m, lane] = matmul(w[pl.ds(m * width, width), lane], src[k], 0, 0).astype(BF)

        each(2, 0, tile)

    tile_rows = width // 2

    def multiply_grads(acts, k, dst):
        for m in range(3):
            src = zs_ref if m == 2 else xs_ref

            def tile(b, m=m, src=src):
                row = pl.multiple_of(b * tile_rows, tile_rows)
                dst[pl.ds(m * width + row, tile_rows)] = matmul(
                    src[k, pl.ds(row, tile_rows)], acts[m], 1, 1
                ).astype(BF)

            each(2, 0, tile)

    def home_grads(h):
        lane = pl.ds(h * half_hidden, half_hidden)
        for m in range(3):
            src = zs_ref if m == 2 else xs_ref

            def tile(b, m=m, src=src):
                row = pl.multiple_of(b * tile_rows, tile_rows)
                at = pl.ds(m * width + row, tile_rows)
                grads[at, lane] = matmul(
                    src[0, pl.ds(row, tile_rows)], home_acts[h, m], 1, 1
                ) + summed[h, at].astype(F32)

            each(2, 0, tile)

    def multiply_rows(w, acts, store):
        def tile(b):
            row = pl.multiple_of(b * tile_rows, tile_rows)
            down = pl.ds(2 * width + row, tile_rows)
            store(row, matmul(w[down], acts[2], 1, 0))
            up = pl.ds(width + row, tile_rows)
            store(
                width + row,
                matmul(w[pl.ds(row, tile_rows)], acts[0], 1, 0)
                + matmul(w[up], acts[1], 1, 0),
            )

        each(2, 0, tile)

    def keep_rows(k):
        def store(row, value):
            rows_acc[k, pl.ds(row, tile_rows)] = value

        return store

    def end_rows(k):
        def store(row, value):
            at = pl.ds(row, tile_rows)
            made[k, at] = (rows_acc[k, at] + value).astype(BF)

        return store

    row_tiles = 2
    tile_columns = count * pair // row_tiles
    tile_sources = count // row_tiles

    def send_rows():
        choose, tokens = ids_t.shape
        ids = jnp.transpose(ids_t[...])
        gates = jnp.transpose(gates_t[...])
        both = jnp.transpose(jnp.concatenate([tokens_t[...], cotangent_t[...]], axis=0))
        slot = lax.broadcasted_iota(jnp.int32, (tokens, 2 * count), 1)
        named = [ids[:, k : k + 1] == slot for k in range(choose)]
        names = sum(jnp.where(hit, 1.0, 0.0) for hit in named)
        square = (tokens, tokens)
        earlier = lax.broadcasted_iota(jnp.int32, square, 0) > lax.broadcasted_iota(
            jnp.int32, square, 1
        )
        turns = matmul(jnp.where(earlier, 1.0, 0.0).astype(BF), names.astype(BF), 1, 0)
        places = []
        for k in range(choose):
            turn = jnp.sum(jnp.where(named[k], turns, 0.0), axis=1, keepdims=True)
            own = ids[:, k : k + 1]
            kind = jnp.where(own >= count, 1, 0)
            places.append(
                (own - kind * count) * pair + kind * capacity + turn.astype(jnp.int32)
            )
        for n in range(row_tiles):
            shape = (tokens, tile_columns)
            column = lax.broadcasted_iota(jnp.int32, shape, 1) + n * tile_columns
            picks = jnp.zeros(shape, F32)
            weight = jnp.zeros(shape, F32)
            for k in range(choose):
                hit = places[k] == column
                picks = picks + jnp.where(hit, 1.0, 0.0)
                weight = weight + jnp.where(hit, gates[:, k : k + 1], 0.0)
            at = pl.ds(n * tile_columns, tile_columns)
            chosen[:, at] = picks.astype(BF)
            top = weight.astype(BF)
            high[:, at] = top
            low[:, at] = (weight - top.astype(F32)).astype(BF)
            plain = matmul(chosen[:, at], both, 0, 0)
            scaled = matmul(high[:, at], both, 0, 0) + matmul(low[:, at], both, 0, 0)
            lane = lax.broadcasted_iota(jnp.int32, plain.shape, 1)
            sent[pl.ds(n * tile_sources, tile_sources)] = (
                jnp.where(lane < width, plain, scaled)
                .astype(BF)
                .reshape(tile_sources, pair, 2 * width)
            )

    def add_rows():
        plain, scaled = 0.0, 0.0
        for n in range(row_tiles):
            at = pl.ds(n * tile_columns, tile_columns)
            block = returned[pl.ds(n * tile_sources, tile_sources)].reshape(
                tile_columns, 2 * width
            )
            plain = plain + matmul(chosen[:, at], block, 1, 0)
            scaled = scaled + (
                matmul(high[:, at], block, 1, 0) + matmul(low[:, at], block, 1, 0)
            )
        output_t[...] = jnp.transpose(scaled)[:width].astype(BF)
        token_grad_t[...] = jnp.transpose(plain)[width:].astype(BF)

    def sort_rows(ref, first_lane, skip):
        sources = 8
        for n in range(rows // 128):
            first = min(128 * n // capacity, count - sources)
            block = got[pl.ds(first, sources), :, pl.ds(first_lane, split)].reshape(
                sources * pair, split
            )
            shape = (sources * pair, 128)
            r = lax.broadcasted_iota(jnp.int32, shape, 0)
            lane = lax.broadcasted_iota(jnp.int32, shape, 1) + 128 * n
            inside = lax.rem(r, pair)
            goes_to = (lax.div(r, pair) + first) * capacity + lax.rem(inside, capacity)
            for k in range(2):
                hit = (goes_to == lane) & (lax.div(inside, capacity) == k)
                tile = matmul(block, jnp.where(hit, 1.0, 0.0).astype(BF), 0, 0)
                ref[k, :, pl.ds(128 * n, 128)] = tile[skip : skip + width].astype(BF)

    def unsort_rows(k, first):
        sources, window = 4, 256
        blocks = count // sources

        def block(b):
            start = lax.min(lax.div(b * sources * capacity, 128) * 128, rows - window)
            start = pl.multiple_of(start, 128)
            shape = (sources * pair, window)
            r = lax.broadcasted_iota(jnp.int32, shape, 0)
            lane = lax.broadcasted_iota(jnp.int32, shape, 1) + start
            inside = lax.rem(r, pair)
            comes_from = (lax.div(r, pair) + b * sources) * capacity + lax.rem(inside, capacity)
            hit = (comes_from == lane) & (lax.div(inside, capacity) == k)
            tile = matmul(
                jnp.where(hit, 1.0, 0.0).astype(BF), made[k, :, pl.ds(start, window)], 1, 1
            ).reshape(sources, pair, 2 * width)
            at = pl.ds(b * sources, sources)
            if first:
                got[at] = tile.astype(BF)
            else:
                got[at] = (got[at].astype(F32) + tile).astype(BF)

        each(blocks, 0, block)

    def over_dp(p, acts, prepare, early, middle, late):
        def rows_of(c, d=None):
            base = lax.rem(c + 2 * ring, ring) * chunk
            if d is None:
                return pl.ds(pl.multiple_of(base, chunk), chunk)
            return pl.ds(pl.multiple_of(base + d * half, half), half)

        def sum_copy(t, m, d):
            c = z + steps - t if d == 0 else z - steps + t
            if t == 0:
                src = parts.at[p, m, rows_of(c, d)]
                dst = landed.at[p, d, 0, m, pl.ds(d * half, half)]
            else:
                src, dst = landed.at[p, d, t - 1, m], landed.at[p, d, t, m]
            return pltpu.make_async_remote_copy(
                src_ref=src,
                dst_ref=dst,
                send_sem=z_send.at[p, d, t, m],
                recv_sem=z_recv.at[p, d, t, m],
                device_id={"dp": right if d == 0 else left},
                device_id_type=MESH,
            )

        def sum_add(t, m, d):
            c = z + steps - t if d == 0 else z - steps + t
            if t == 1:
                mine, other = pl.ds(d * half, half), pl.ds((1 - d) * half, half)
                landed[p, d, 0, m, mine] = (
                    landed[p, d, 0, m, mine].astype(F32) + parts[p, m, rows_of(c, d)].astype(F32)
                ).astype(BF)
                landed[p, d, 0, m, other] = parts[p, m, rows_of(c, 1 - d)]
            else:
                landed[p, d, t - 1, m] = (
                    landed[p, d, t - 1, m].astype(F32) + parts[p, m, rows_of(c)].astype(F32)
                ).astype(BF)

        def spread_copy(t, m, d):
            c = z - t if d == 0 else z + t
            at = rows_of(c, d) if t == steps - 1 else rows_of(c)
            return pltpu.make_async_remote_copy(
                src_ref=acts.at[m, at],
                dst_ref=acts.at[m, at],
                send_sem=g_send.at[p, d, t, m],
                recv_sem=g_recv.at[p, d, t, m],
                device_id={"dp": right if d == 0 else left},
                device_id_type=MESH,
            )

        in_flight = ([], [])

        def launch(copy, d):
            if len(in_flight[d]) == DEPTH:
                in_flight[d].pop(0).wait_send()
            copy.start()
            in_flight[d].append(copy)

        for m in range(3):
            prepare(m)
            for d in sides:
                launch(sum_copy(0, m, d), d)
        early()
        for t in range(1, steps):
            for m in range(3):
                for d in sides:
                    sum_copy(t - 1, m, d).wait_recv()
                    sum_add(t, m, d)
                    launch(sum_copy(t, m, d), d)

        def total(m):
            for d in sides:
                sum_copy(steps - 1, m, d).wait_recv()
            return (
                landed[p, 0, steps - 1, m].astype(F32)
                + landed[p, 1, steps - 1, m].astype(F32)
                + parts[p, m, rows_of(z)].astype(F32)
            )

        def spread_first(m, value):
            acts[m, rows_of(z)] = value.astype(BF)
            for d in sides:
                launch(spread_copy(0, m, d), d)

        gate = total(0)
        up = total(1)
        q = jax.nn.sigmoid(gate)
        silu = gate * q
        spread_first(2, silu * up)
        grad = total(2)
        spread_first(0, grad * up * q * (1.0 + gate * (1.0 - q)))
        spread_first(1, grad * silu)
        middle()
        for t in range(1, steps):
            for m in (2, 0, 1):
                for d in sides:
                    spread_copy(t - 1, m, d).wait_recv()
                    launch(spread_copy(t, m, d), d)
            if t in late:
                late[t]()
        for m in (2, 0, 1):
            for d in sides:
                spread_copy(steps - 1, m, d).wait_recv()
        for d in sides:
            for copy in in_flight[d]:
                copy.wait_send()

    def nothing():
        pass

    moves = [
        Move(0, weights.at[0], copied.at[0], False),
        Move(1, weights.at[1], copied.at[1], False),
        Move(2, slot_grads.at[0], summed.at[0], True),
        Move(3, slot_grads.at[1], summed.at[1], True),
    ]
    for m in range(3):
        place_copy(0, m).wait()
    moves[0].begin(1, count // 2)
    send_rows()
    exchange(sent, got, 0, 0, split)()
    others = exchange(sent, got, 1, split)

    def first_inputs(m):
        if m == 0:
            sort_rows(xs_ref, 0, 0)
        if m == 2:
            others()
            sort_rows(zs_ref, 2 * width - split, split - width)
        multiply_part(weights.at[0], 0, 0, m)

    def more_weights():
        moves[0].begin(count // 2, count)
        for m in range(3):
            place_copy(1, m).wait()

    over_dp(0, home_acts.at[0], first_inputs, more_weights, moves[0].pass_on, {})
    moves[0].finish()
    moves[1].begin()
    over_dp(
        1,
        rep_acts.at[0],
        lambda m: multiply_part(copied.at[0], 1, 1, m),
        nothing,
        moves[1].pass_on,
        {1: lambda: multiply_rows(weights.at[0], home_acts.at[0], keep_rows(0))},
    )
    moves[1].finish()

    def first_grads():
        multiply_grads(rep_acts.at[0], 1, slot_grads.at[0])
        moves[2].begin()

    over_dp(
        0,
        rep_acts.at[1],
        lambda m: multiply_part(copied.at[1], 1, 0, m),
        first_grads,
        moves[2].pass_on,
        {1: lambda: multiply_rows(copied.at[0], rep_acts.at[0], keep_rows(1))},
    )

    def second_grads():
        moves[2].finish()
        multiply_grads(rep_acts.at[1], 1, slot_grads.at[1])
        moves[3].begin()

    over_dp(
        1,
        home_acts.at[1],
        lambda m: multiply_part(weights.at[1], 0, 1, m),
        second_grads,
        moves[3].pass_on,
        {
            1: lambda: multiply_rows(copied.at[1], rep_acts.at[1], end_rows(1)),
            2: lambda: unsort_rows(1, True),
        },
    )
    multiply_rows(weights.at[1], home_acts.at[1], end_rows(0))
    unsort_rows(0, False)
    done = exchange(got, returned, 2)
    home_grads(0)
    moves[3].finish()
    home_grads(1)
    done()
    add_rows()


def layer(
    plan, before_it, last_of, ids_t, gates_t, tokens_t, cotangent_t, w_gate, w_up, w_down, capacity, ring
):
    count = plan.shape[0]
    tokens = ids_t.shape[1]
    width, hidden = w_gate.shape
    two_width = 2 * width
    half_hidden = hidden // 2
    pair = 2 * capacity
    rows = count * capacity
    columns = count * pair
    flat = -(-3 * width // (8 * 16)) * 8 * 16
    steps = ring // 2
    chunk = half_hidden // ring
    piece = (flat // 8, half_hidden * 8 // count)
    sem = pltpu.SemaphoreType.DMA
    acts = (2, 3, half_hidden, rows)
    halves = (2, flat, half_hidden)
    blocks = (count, pair, two_width)
    return pl.pallas_call(
        functools.partial(layer_kernel, count, ring, capacity),
        out_shape=(
            jax.ShapeDtypeStruct((width, tokens), BF),
            jax.ShapeDtypeStruct((width, tokens), BF),
            jax.ShapeDtypeStruct((3 * width, hidden), F32),
        ),
        in_specs=[pl.BlockSpec(memory_space=pltpu.SMEM)] * 3
        + [pl.BlockSpec(memory_space=VMEM)] * 4
        + [pl.BlockSpec(memory_space=pl.ANY)] * 3,
        out_specs=[pl.BlockSpec(memory_space=VMEM)] * 3,
        scratch_shapes=[
            VMEM(halves, BF),
            VMEM(blocks, BF),
            VMEM(blocks, BF),
            VMEM((tokens, columns), BF),
            VMEM((tokens, columns), BF),
            VMEM((tokens, columns), BF),
            VMEM(blocks, BF),
            VMEM(acts, BF),
            VMEM(halves, BF),
            VMEM((2, width, rows), BF),
            VMEM((2, width, rows), BF),
            VMEM(halves, BF),
            VMEM((2, 3, half_hidden, rows), BF),
            VMEM(acts, BF),
            VMEM((2, 2, steps, 3, chunk, rows), BF),
            VMEM((count,) + piece, BF),
            VMEM((count,) + piece, BF),
            VMEM((2, count) + piece, BF),
            VMEM((count,) + piece, F32),
            VMEM(halves, BF),
            VMEM((2, two_width, rows), F32),
            VMEM((2, two_width, rows), BF),
            sem((2, 2, steps, 3)),
            sem((2, 2, steps, 3)),
            sem((2, 2, steps, 3)),
            sem((2, 2, steps, 3)),
            sem((2, count)),
            sem((2, count)),
            sem((2, count)),
            sem((2, count)),
            sem((3, count)),
            sem((3, count)),
            sem((5,)),
            sem((2, 3)),
        ],
        compiler_params=pltpu.CompilerParams(
            collective_id=1, has_side_effects=True, vmem_limit_bytes=63 << 20
        ),
        name="layer",
    )(plan, before_it, last_of, ids_t, gates_t, tokens_t, cotangent_t, w_gate, w_up, w_down)


def body(tokens, cotangent, slot_ids, gates, plan, w_gate, w_up, w_down):
    count = lax.axis_size("expert")
    ring = lax.axis_size("dp")
    token_count, width = tokens.shape
    capacity = 5 * token_count * slot_ids.shape[1] // (4 * 2 * count)

    s_ids = jnp.arange(count, dtype=jnp.int32)
    alike = (plan[None, :] == plan[:, None]) & (s_ids[None, :] < s_ids[:, None])
    before_it = jnp.max(jnp.where(alike, s_ids[None, :], -1), axis=1)
    last_of = jnp.max(jnp.where(plan[None, :] == s_ids[:, None], s_ids[None, :], -1), axis=1)

    output_t, token_grad_t, grads = layer(
        plan,
        before_it,
        last_of,
        slot_ids.T,
        gates.T,
        tokens.T,
        cotangent.T,
        w_gate[0],
        w_up[0],
        jnp.swapaxes(w_down[0], 0, 1),
        capacity,
        ring,
    )
    return (
        output_t.T,
        token_grad_t.T,
        grads[:width][None],
        grads[width : 2 * width][None],
        jnp.swapaxes(grads[2 * width :], 0, 1)[None],
    )


def solution(mesh):
    in_specs = (
        P("expert", "dp"),
        P("expert", "dp"),
        P("expert", None),
        P("expert", None),
        P(),
        P("expert", "dp", None),
        P("expert", "dp", None),
        P("expert", None, "dp"),
    )
    out_specs = (
        P("expert", "dp"),
        P("expert", "dp"),
        P("expert", "dp", None),
        P("expert", "dp", None),
        P("expert", None, "dp"),
    )
    return jax.shard_map(body, mesh=mesh, in_specs=in_specs, out_specs=out_specs, check_vma=False)
```
